512 devices in a mesh: dp: 4 (over x_lo, core), blk: 128 (over y, z, x_hi).
Axes of the slice: x: 4 (x_hi: 2, x_lo: 2; x = x_hi * 2 + x_lo), y: 8, z: 8, core: 2. Of those that a mesh axis runs over, the one named last changes fastest.
Arguments:
- queries: bfloat16 [4, 24576, 512], P('dp', 'blk'), may hold values from -6 to 6, as said below
- key_in: bfloat16 [4, 24576, 512], P('dp', 'blk'), may hold values from -6 to 6, as said below
- value_in: bfloat16 [4, 24576, 512], P('dp', 'blk'), may hold values from -6 to 6
- out_weight: bfloat16 [512, 1024], replicated, may hold values from -2 to 2
- conv_kernel: float32 [31, 1024], replicated, may hold values from -1 to 1
- cotangent: bfloat16 [4, 24576, 1024], P('dp', 'blk'), may hold values from -6 to 6
Outputs:
- out_frames: bfloat16 [4, 24576, 1024], P('dp', 'blk')
- query_grad: bfloat16 [4, 24576, 512], P('dp', 'blk')
- key_grad: bfloat16 [4, 24576, 512], P('dp', 'blk')
- value_grad: bfloat16 [4, 24576, 512], P('dp', 'blk')
- weight_grad: float32 [512, 1024], replicated
- kernel_grad: float32 [31, 1024], replicated
The draws below stay inside these ranges and needn't reach their ends.
Inputs may be any that keep to these rules, and one draw needn't show every extreme that they name: `queries`: independent entries. `key_in`: independent entries.
All inputs are finite; a program needn't handle non-finite values.
Results may differ from the reference program's by a relative error of at most 0.024.
Values may be sent and summed in bfloat16 or wider, within the bound.
A program may use at most 64 MiB of HBM per device.

```python
import math
import jax
import jax.numpy as jnp
from jax import lax

D = 1024
ATT_HEADS = 8
HEAD_DIM = 64
KW = 31
BLOCK = 96
CTX = 3
ATT = 512
SEQS = 4
FRAMES = 24576


def drawn_rows(key):
    base = jax.random.normal(key, (SEQS, FRAMES, ATT), jnp.float32)
    return jnp.clip(base, -6.0, 6.0)


def draw_queries(key, part):
    base = drawn_rows(jax.random.fold_in(key, 1))
    return base.astype(jnp.bfloat16)


def draw_key_in(key, part):
    base = drawn_rows(jax.random.fold_in(key, 2))
    return base.astype(jnp.bfloat16)


def levels(stream_key, dims, split, smallest, top_value):
    gain = 1.0
    for axis_at, parts in split:
        heights = jax.random.uniform(jax.random.fold_in(jax.random.fold_in(stream_key, 6), axis_at), (parts,), jnp.float32, smallest / len(split), top_value / len(split))
        gain = gain * jnp.repeat(jnp.exp(heights), dims[axis_at] // parts).reshape((-1,) + (1,) * (len(dims) - 1 - axis_at))
    return gain


def bell_draw(key, shape, width, reach, split=(), kind=jnp.bfloat16):
    drawn = width * jax.random.normal(key, shape, jnp.float32)
    if split:
        drawn = drawn * levels(key, shape, split, -0.22, 0.18)
    return jnp.clip(drawn, -reach, reach).astype(kind)


def setup_inputs(seed: int = 0) -> dict:
    seeds = jax.random.split(jax.random.key(seed), 7)
    queries = draw_queries(jax.random.fold_in(seeds[6], 71), 0)
    key_in = draw_key_in(jax.random.fold_in(seeds[6], 71), 0)
    value_in = bell_draw(seeds[2], (SEQS, FRAMES, ATT), 1.0, 6.0, ((0, 4), (1, 128)))
    out_weight = bell_draw(seeds[3], (ATT, D), (HEAD_DIM // 8) ** -0.5, 2.0)
    conv_kernel = bell_draw(seeds[4], (KW, D), KW ** -0.5, 1.0, (), jnp.float32)
    cotangent = bell_draw(seeds[5], (SEQS, FRAMES, D), 1.0, 6.0, ((0, 4), (1, 128)))
    return {"queries": queries, "key_in": key_in, "value_in": value_in, "out_weight": out_weight, "conv_kernel": conv_kernel, "cotangent": cotangent}


NEGATIVE = -1e+30

def rounded(field):
    return lax.optimization_barrier(field.astype(jnp.bfloat16)).astype(jnp.float32)

def window_scores(query_block, key_block, start, left_span, score_scale):
    pair_len = query_block.shape[0]
    query_pos = start + jnp.arange(pair_len, dtype=jnp.int32)
    key_pos = start - left_span + jnp.arange(left_span + pair_len, dtype=jnp.int32)
    distance = query_pos[:, None] - key_pos[None, :]
    visible = (distance >= 0) & (distance < left_span) & (key_pos[None, :] >= 0)
    scores = jnp.einsum('qhd,khd->hqk', query_block.astype(jnp.float32), key_block.astype(jnp.float32)) * score_scale
    return (jnp.where(visible[None], scores, NEGATIVE), visible[None])

def attend(queries, keys_seq, values_seq, left_span, score_scale):
    pair_len = 2 * BLOCK
    key_pad = jnp.pad(keys_seq, ((left_span, 0), (0, 0), (0, 0)))
    value_pad = jnp.pad(values_seq, ((left_span, 0), (0, 0), (0, 0)))

    def one_block(block_id):
        start = block_id * pair_len
        query_block = lax.dynamic_slice_in_dim(queries, start, pair_len, 0)
        key_block = lax.dynamic_slice_in_dim(key_pad, start, left_span + pair_len, 0)
        value_block = lax.dynamic_slice_in_dim(value_pad, start, left_span + pair_len, 0)
        scores, visible = window_scores(query_block, key_block, start, left_span, score_scale)
        row_max = lax.optimization_barrier(jnp.max(scores, axis=-1, keepdims=True))
        weights = jnp.where(visible, jnp.exp(scores - row_max), 0.0)
        row_sum = lax.optimization_barrier(jnp.sum(weights, axis=-1, keepdims=True))
        mixed = jnp.einsum('hqk,khd->hqd', rounded(weights), value_block.astype(jnp.float32)) / row_sum
        return (jnp.transpose(mixed, (1, 0, 2)).astype(jnp.bfloat16), (row_max + jnp.log(row_sum))[..., 0])
    attended, log_sums = lax.map(one_block, jnp.arange(FRAMES // pair_len, dtype=jnp.int32))
    return (attended.reshape(FRAMES, ATT_HEADS, HEAD_DIM), log_sums)

def attend_back(queries, keys_seq, values_seq, dattended, log_sums, deltas, left_span, score_scale):
    pair_len = 2 * BLOCK
    span_len = left_span + pair_len
    key_pad = jnp.pad(keys_seq, ((left_span, 0), (0, 0), (0, 0)))
    value_pad = jnp.pad(values_seq, ((left_span, 0), (0, 0), (0, 0)))
    zero_pad = jnp.zeros((FRAMES + left_span, ATT_HEADS, HEAD_DIM), jnp.float32)

    def one_block(carry, block_id):
        dkey_pad, dvalue_pad = carry
        start = block_id * pair_len
        query_block = lax.dynamic_slice_in_dim(queries, start, pair_len, 0).astype(jnp.float32)
        dout_block = lax.dynamic_slice_in_dim(dattended, start, pair_len, 0).astype(jnp.float32)
        key_block = lax.dynamic_slice_in_dim(key_pad, start, span_len, 0)
        value_block = lax.dynamic_slice_in_dim(value_pad, start, span_len, 0).astype(jnp.float32)
        scores, visible = window_scores(query_block, key_block, start, left_span, score_scale)
        probs = jnp.where(visible, jnp.exp(scores - log_sums[block_id][..., None]), 0.0)
        dvalue_block = jnp.einsum('hqk,qhd->khd', rounded(probs), dout_block)
        dprobs = jnp.einsum('qhd,khd->hqk', dout_block, value_block)
        dscores = rounded(probs * (dprobs - deltas[block_id][..., None]))
        dquery_block = jnp.einsum('hqk,khd->qhd', dscores, key_block.astype(jnp.float32)) * score_scale
        dkey_block = jnp.einsum('hqk,qhd->khd', dscores, query_block) * score_scale
        dkey_pad = lax.dynamic_update_slice_in_dim(dkey_pad, lax.dynamic_slice_in_dim(dkey_pad, start, span_len, 0) + dkey_block, start, 0)
        dvalue_pad = lax.dynamic_update_slice_in_dim(dvalue_pad, lax.dynamic_slice_in_dim(dvalue_pad, start, span_len, 0) + dvalue_block, start, 0)
        return ((dkey_pad, dvalue_pad), dquery_block.astype(jnp.bfloat16))
    (dkey_pad, dvalue_pad), dquery = lax.scan(one_block, (zero_pad, zero_pad), jnp.arange(FRAMES // pair_len, dtype=jnp.int32))
    return (dquery.reshape(FRAMES, ATT), dkey_pad[left_span:].astype(jnp.bfloat16).reshape(FRAMES, ATT), dvalue_pad[left_span:].astype(jnp.bfloat16).reshape(FRAMES, ATT))

def conv_forward(hidden, conv_kernel):
    hidden_pad = jnp.pad(hidden, ((KW - 1, 0), (0, 0)))

    def add_tap(tap_index, running):
        return running + conv_kernel[tap_index] * lax.dynamic_slice_in_dim(hidden_pad, KW - 1 - tap_index, FRAMES, 0)
    return (lax.fori_loop(0, KW, add_tap, jnp.zeros_like(hidden)), hidden_pad)

def conv_back(dmixed, hidden_pad, conv_kernel):
    dmixed_pad = jnp.pad(dmixed, ((0, KW - 1), (0, 0)))

    def add_tap(tap_index, running):
        return running + conv_kernel[tap_index] * lax.dynamic_slice_in_dim(dmixed_pad, tap_index, FRAMES, 0)
    dhidden = lax.fori_loop(0, KW, add_tap, jnp.zeros_like(dmixed))

    def kernel_tap(tap_index):
        return lax.optimization_barrier(jnp.sum(dmixed * lax.dynamic_slice_in_dim(hidden_pad, KW - 1 - tap_index, FRAMES, 0), axis=0))
    return (dhidden, lax.map(kernel_tap, jnp.arange(KW, dtype=jnp.int32)))

def reference(queries, key_in, value_in, out_weight, conv_kernel, cotangent):
    score_scale = 1.0 / math.sqrt(HEAD_DIM)
    left_span = CTX * 2 * BLOCK

    def one_sequence(items):
        query_seq, key_seq, value_seq, grad_seq = items
        query_nat = query_seq.reshape(FRAMES, ATT_HEADS, HEAD_DIM)
        key_nat = key_seq.reshape(FRAMES, ATT_HEADS, HEAD_DIM)
        value_nat = value_seq.reshape(FRAMES, ATT_HEADS, HEAD_DIM)
        attended, log_sums = attend(query_nat, key_nat, value_nat, left_span, score_scale)
        flat = attended.reshape(FRAMES, ATT)
        hidden = jnp.dot(flat, out_weight, preferred_element_type=jnp.float32).astype(jnp.bfloat16)
        mixed, hidden_pad = conv_forward(hidden.astype(jnp.float32), conv_kernel)
        sigma = jax.nn.sigmoid(mixed)
        out_nat = (mixed * sigma).astype(jnp.bfloat16)
        grad_nat = grad_seq.astype(jnp.float32)
        dmixed = grad_nat * sigma * (1.0 + mixed * (1.0 - sigma))
        dhidden, kernel_term = conv_back(dmixed, hidden_pad, conv_kernel)
        dhidden = dhidden.astype(jnp.bfloat16)
        dattended = jnp.dot(dhidden, out_weight.T, preferred_element_type=jnp.float32).astype(jnp.bfloat16)
        weight_term = jnp.dot(flat.T, dhidden, preferred_element_type=jnp.float32)
        dattended = dattended.reshape(FRAMES, ATT_HEADS, HEAD_DIM)
        delta_flat = jnp.einsum('qhd,qhd->hq', dattended.astype(jnp.float32), attended.astype(jnp.float32))
        deltas = jnp.transpose(delta_flat.reshape(ATT_HEADS, FRAMES // (2 * BLOCK), 2 * BLOCK), (1, 0, 2))
        dquery, dkey, dvalue = attend_back(query_nat, key_nat, value_nat, dattended, log_sums, deltas, left_span, score_scale)
        return (out_nat, dquery, dkey, dvalue, weight_term, kernel_term)
    results = lax.map(one_sequence, (queries, key_in, value_in, cotangent))
    return (results[0], results[1], results[2], results[3], lax.optimization_barrier(jnp.sum(results[4], axis=0)), lax.optimization_barrier(jnp.sum(results[5], axis=0)))
```

```python
import math

import jax
import jax.numpy as jnp
from jax import lax
from jax.sharding import PartitionSpec as P

ATT_HEADS = 8
HEAD_DIM = 64
CTX_MAX = 3
ATT = 512


NEGATIVE = -1e30


def from_behind(block, axis, distance):
    devices = range(lax.axis_size(axis))
    route = [(i - distance, i) for i in devices if i - distance in devices]
    return lax.ppermute(block, axis, route)


def split_heads(matrix):
    return matrix.reshape(matrix.shape[0], ATT_HEADS, HEAD_DIM)


def depthwise(extended, conv_kernel, row_count, ahead):
    tap_count = conv_kernel.shape[0]
    total = None
    for tap_index in range(tap_count):
        first_row = tap_index if ahead else tap_count - 1 - tap_index
        term = conv_kernel[tap_index] * extended[first_row:first_row + row_count]
        total = term if total is None else total + term
    return total


def sum_weights(weight_part, kernel_part):
    return lax.psum((weight_part, kernel_part), ("dp", "blk"))


def per_device(queries, key_in, value_in, out_weight, conv_kernel, cotangent):
    cycle_count = lax.axis_size("blk")
    device = lax.axis_index("blk")
    row_count = queries.shape[1]
    context = min(CTX_MAX, cycle_count // 4)
    left_span = context * row_count
    score_scale = 1.0 / math.sqrt(HEAD_DIM)
    edge_rows = conv_kernel.shape[0] - 1
    row_ids = jnp.arange(row_count, dtype=jnp.int32)
    query_heads = split_heads(queries[0])
    own_tile = jnp.concatenate([key_in[0], value_in[0]], axis=1)
    own_pos = device * row_count + row_ids

    offsets = list(range(context, 0, -1))
    window = jnp.concatenate(
        [from_behind(own_tile, "blk", offset) for offset in offsets] + [own_tile], axis=0
    )
    key_pos = jnp.concatenate([(device - offset) * row_count + row_ids for offset in offsets] + [own_pos])
    distance = own_pos[:, None] - key_pos[None, :]
    visible = ((distance >= 0) & (distance < left_span) & (key_pos[None, :] >= 0))[None]
    key_heads = split_heads(window[:, :ATT])
    value_heads = split_heads(window[:, ATT:])

    scores = (
        jnp.einsum("qhd,khd->hqk", query_heads, key_heads, preferred_element_type=jnp.float32)
        * score_scale
    )
    scores = jnp.where(visible, scores, NEGATIVE)
    row_max = jnp.max(scores, axis=-1)
    weights = jnp.where(visible, jnp.exp(scores - row_max[..., None]), 0.0)
    row_sum = jnp.sum(weights, axis=-1)
    weighted = jnp.einsum(
        "hqk,khd->qhd", weights.astype(jnp.bfloat16), value_heads, preferred_element_type=jnp.float32
    )
    attended = (weighted / jnp.transpose(row_sum)[:, :, None]).astype(jnp.bfloat16)
    log_sums = row_max + jnp.log(row_sum)
    flat = attended.reshape(row_count, ATT)

    hidden = jnp.dot(flat, out_weight, preferred_element_type=jnp.float32).astype(jnp.bfloat16)
    before = from_behind(hidden[-edge_rows:], "blk", 1)
    extended = jnp.concatenate([before, hidden], axis=0).astype(jnp.float32)
    mixed = depthwise(extended, conv_kernel, row_count, False)
    sigma = jax.nn.sigmoid(mixed)
    out_frames = (mixed * sigma).astype(jnp.bfloat16)[None]
    upstream = cotangent[0].astype(jnp.float32)
    dmixed = upstream * sigma * (1.0 + mixed * (1.0 - sigma))
    after = from_behind(dmixed[:edge_rows].astype(jnp.bfloat16), "blk", -1).astype(jnp.float32)
    dextended = jnp.concatenate([dmixed, after], axis=0)
    dhidden = depthwise(dextended, conv_kernel, row_count, True).astype(jnp.bfloat16)

    kernel_part = jnp.stack(
        [
            jnp.sum(dmixed * extended[edge_rows - tap:edge_rows - tap + row_count], axis=0)
            for tap in range(edge_rows + 1)
        ]
    )
    weight_part = jnp.einsum("ra,rd->ad", flat, dhidden, preferred_element_type=jnp.float32)
    weight_total, kernel_total = sum_weights(weight_part, kernel_part)

    dattended = jnp.einsum(
        "rd,ad->ra", dhidden, out_weight, preferred_element_type=jnp.float32
    ).astype(jnp.bfloat16)
    dout_heads = split_heads(dattended)
    deltas = jnp.einsum("rhe,rhe->hr", dout_heads, attended, preferred_element_type=jnp.float32)

    probs = jnp.where(visible, jnp.exp(scores - log_sums[..., None]), 0.0)
    dvalue_heads = jnp.einsum(
        "hqk,qhd->khd", probs.astype(jnp.bfloat16), dout_heads, preferred_element_type=jnp.float32
    )
    dprobs = jnp.einsum("qhd,khd->hqk", dout_heads, value_heads, preferred_element_type=jnp.float32)
    dscores = (probs * (dprobs - deltas[..., None])).astype(jnp.bfloat16)
    dquery = (
        jnp.einsum("hqk,khd->qhd", dscores, key_heads, preferred_element_type=jnp.float32)
        * score_scale
    )
    dkey_heads = (
        jnp.einsum("hqk,qhd->khd", dscores, query_heads, preferred_element_type=jnp.float32)
        * score_scale
    )
    window_rows = window.shape[0]
    dkv = jnp.concatenate(
        [dkey_heads.reshape(window_rows, ATT), dvalue_heads.reshape(window_rows, ATT)], axis=1
    )
    dkv_total = dkv[context * row_count:]
    for slot, offset in enumerate(offsets):
        part = dkv[slot * row_count:(slot + 1) * row_count].astype(jnp.bfloat16)
        dkv_total = dkv_total + from_behind(part, "blk", -offset).astype(jnp.float32)

    query_grad = dquery.reshape(row_count, ATT).astype(jnp.bfloat16)[None]
    key_grad = dkv_total[:, :ATT].astype(jnp.bfloat16)[None]
    value_grad = dkv_total[:, ATT:].astype(jnp.bfloat16)[None]
    return (out_frames, query_grad, key_grad, value_grad, weight_total, kernel_total)


def solution(mesh):
    return jax.shard_map(
        per_device,
        mesh=mesh,
        in_specs=(
            P("dp", "blk", None),
            P("dp", "blk", None),
            P("dp", "blk", None),
            P(),
            P(),
            P("dp", "blk", None),
        ),
        out_specs=(
            P("dp", "blk", None),
            P("dp", "blk", None),
            P("dp", "blk", None),
            P("dp", "blk", None),
            P(),
            P(),
        ),
        check_vma=False,
    )
```

```python
import functools
import math

import jax
import jax.numpy as jnp
from jax import lax
from jax.experimental import pallas as pl
from jax.experimental.pallas import tpu as pltpu
from jax.sharding import PartitionSpec as P

ATT_HEADS = 8
HEAD_DIM = 64
CTX_MAX = 3
ATT = 512


NEGATIVE = -1e30
MESH_ID = pl.DeviceIdType.MESH


def reduce_bits(dp_size, blk_size):
    if dp_size == 4 and blk_size == 128:
        return [("dp", 1), ("dp", 2), ("blk", 16), ("blk", 2), ("blk", 32),
                ("blk", 4), ("blk", 64), ("blk", 8), ("blk", 1)]
    bits = []
    for axis, size in (("dp", dp_size), ("blk", blk_size)):
        m = 1
        while m < size:
            bits.append((axis, m))
            m *= 2
    return bits


def allreduce_kernel(bits, n_halve, x_ref, o_ref, *scratch):
    halves = scratch[:n_halve]
    doubles = scratch[n_halve:len(bits)]
    acc, send_sem, recv_sem = scratch[len(bits):]
    me = {"dp": lax.axis_index("dp"), "blk": lax.axis_index("blk")}

    def partner(axis, m):
        bit = (me[axis] // m) % 2
        peer = me[axis] + m - 2 * m * bit
        ids = (peer, me["blk"]) if axis == "dp" else (me["dp"], peer)
        return bit, ids

    barrier = pltpu.get_barrier_semaphore()
    for axis, m in bits:
        pl.semaphore_signal(barrier, 1, device_id=partner(axis, m)[1], device_id_type=MESH_ID)
    pl.semaphore_wait(barrier, len(bits))

    offset = 0
    length = o_ref.shape[0]
    plan = []
    for step in range(n_halve):
        axis, m = bits[step]
        half = length // 2
        bit, ids = partner(axis, m)
        keep = offset + bit * half
        give = offset + (1 - bit) * half
        source = x_ref if step == 0 else acc
        copy = pltpu.make_async_remote_copy(
            src_ref=source.at[pl.ds(give, half)], dst_ref=halves[step],
            send_sem=send_sem.at[step], recv_sem=recv_sem.at[step],
            device_id=ids, device_id_type=MESH_ID)
        copy.start()
        copy.wait()
        acc[pl.ds(keep, half)] = source[pl.ds(keep, half)] + halves[step][...]
        plan.append((ids, keep, half))
        offset, length = keep, half
    for slot, (axis, m) in enumerate(bits[n_halve:]):
        step = n_halve + slot
        bit, ids = partner(axis, m)
        copy = pltpu.make_async_remote_copy(
            src_ref=acc.at[pl.ds(offset, length)], dst_ref=doubles[slot],
            send_sem=send_sem.at[step], recv_sem=recv_sem.at[step],
            device_id=ids, device_id_type=MESH_ID)
        copy.start()
        copy.wait()
        acc[pl.ds(offset, length)] = acc[pl.ds(offset, length)] + doubles[slot][...]
    o_ref[pl.ds(offset, length)] = acc[pl.ds(offset, length)]
    for back, (ids, keep, half) in enumerate(reversed(plan)):
        step = len(bits) + back
        copy = pltpu.make_async_remote_copy(
            src_ref=o_ref.at[pl.ds(keep, half)], dst_ref=o_ref.at[pl.ds(keep, half)],
            send_sem=send_sem.at[step], recv_sem=recv_sem.at[step],
            device_id=ids, device_id_type=MESH_ID)
        copy.start()
        copy.wait()


def allreduce(x, dp_size, blk_size, n_halve_max=5):
    bits = reduce_bits(dp_size, blk_size)
    rows = x.shape[0]
    n_halve = 0
    while n_halve < min(n_halve_max, len(bits)) and rows % (2 ** (n_halve + 1)) == 0:
        n_halve += 1
    lengths = [rows // 2 ** (s + 1) for s in range(n_halve)]
    final = rows // 2 ** n_halve
    tile = x.shape[1:]
    scratch = [pltpu.VMEM((n,) + tile, x.dtype) for n in lengths]
    scratch += [pltpu.VMEM((final,) + tile, x.dtype) for _ in bits[n_halve:]]
    steps = len(bits) + n_halve
    scratch += [pltpu.VMEM(x.shape, x.dtype), pltpu.SemaphoreType.DMA((steps,)), pltpu.SemaphoreType.DMA((steps,))]
    return pl.pallas_call(
        functools.partial(allreduce_kernel, bits, n_halve),
        out_shape=jax.ShapeDtypeStruct(x.shape, x.dtype),
        in_specs=[pl.BlockSpec(memory_space=pltpu.VMEM)],
        out_specs=pl.BlockSpec(memory_space=pltpu.VMEM),
        scratch_shapes=scratch,
        compiler_params=pltpu.CompilerParams(collective_id=0, has_side_effects=True),
    )(x)


def from_behind(block, axis, distance):
    devices = range(lax.axis_size(axis))
    route = [(i - distance, i) for i in devices if i - distance in devices]
    return lax.ppermute(block, axis, route)


def split_heads(matrix):
    return matrix.reshape(matrix.shape[0], ATT_HEADS, HEAD_DIM)


def depthwise(extended, conv_kernel, row_count, ahead):
    tap_count = conv_kernel.shape[0]
    total = None
    for tap_index in range(tap_count):
        first_row = tap_index if ahead else tap_count - 1 - tap_index
        term = conv_kernel[tap_index] * extended[first_row:first_row + row_count]
        total = term if total is None else total + term
    return total


def sum_weights(weight_part, kernel_part):
    width = weight_part.shape[1]
    rows = weight_part.shape[0] + kernel_part.shape[0]
    padded = -(-rows // 32) * 32
    packed = jnp.concatenate(
        [weight_part, kernel_part, jnp.zeros((padded - rows, width), jnp.float32)], axis=0
    )
    total = allreduce(
        packed.reshape(padded, 8, width // 8),
        lax.axis_size("dp"),
        lax.axis_size("blk"),
    ).reshape(padded, width)
    return total[: weight_part.shape[0]], total[weight_part.shape[0] : rows]


def per_device(queries, key_in, value_in, out_weight, conv_kernel, cotangent):
    cycle_count = lax.axis_size("blk")
    device = lax.axis_index("blk")
    row_count = queries.shape[1]
    context = min(CTX_MAX, cycle_count // 4)
    left_span = context * row_count
    score_scale = 1.0 / math.sqrt(HEAD_DIM)
    edge_rows = conv_kernel.shape[0] - 1
    row_ids = jnp.arange(row_count, dtype=jnp.int32)
    query_heads = split_heads(queries[0])
    own_tile = jnp.concatenate([key_in[0], value_in[0]], axis=1)
    own_pos = device * row_count + row_ids

    offsets = list(range(context, 0, -1))
    window = jnp.concatenate(
        [from_behind(own_tile, "blk", offset) for offset in offsets] + [own_tile], axis=0
    )
    key_pos = jnp.concatenate([(device - offset) * row_count + row_ids for offset in offsets] + [own_pos])
    distance = own_pos[:, None] - key_pos[None, :]
    visible = ((distance >= 0) & (distance < left_span) & (key_pos[None, :] >= 0))[None]
    key_heads = split_heads(window[:, :ATT])
    value_heads = split_heads(window[:, ATT:])

    scores = (
        jnp.einsum("qhd,khd->hqk", query_heads, key_heads, preferred_element_type=jnp.float32)
        * score_scale
    )
    scores = jnp.where(visible, scores, NEGATIVE)
    row_max = jnp.max(scores, axis=-1)
    weights = jnp.where(visible, jnp.exp(scores - row_max[..., None]), 0.0)
    row_sum = jnp.sum(weights, axis=-1)
    weighted = jnp.einsum(
        "hqk,khd->qhd", weights.astype(jnp.bfloat16), value_heads, preferred_element_type=jnp.float32
    )
    attended = (weighted / jnp.transpose(row_sum)[:, :, None]).astype(jnp.bfloat16)
    log_sums = row_max + jnp.log(row_sum)
    flat = attended.reshape(row_count, ATT)

    hidden = jnp.dot(flat, out_weight, preferred_element_type=jnp.float32).astype(jnp.bfloat16)
    before = from_behind(hidden[-edge_rows:], "blk", 1)
    extended = jnp.concatenate([before, hidden], axis=0).astype(jnp.float32)
    mixed = depthwise(extended, conv_kernel, row_count, False)
    sigma = jax.nn.sigmoid(mixed)
    out_frames = (mixed * sigma).astype(jnp.bfloat16)[None]
    upstream = cotangent[0].astype(jnp.float32)
    dmixed = upstream * sigma * (1.0 + mixed * (1.0 - sigma))
    after = from_behind(dmixed[:edge_rows].astype(jnp.bfloat16), "blk", -1).astype(jnp.float32)
    dextended = jnp.concatenate([dmixed, after], axis=0)
    dhidden = depthwise(dextended, conv_kernel, row_count, True).astype(jnp.bfloat16)

    kernel_part = jnp.stack(
        [
            jnp.sum(dmixed * extended[edge_rows - tap:edge_rows - tap + row_count], axis=0)
            for tap in range(edge_rows + 1)
        ]
    )
    weight_part = jnp.einsum("ra,rd->ad", flat, dhidden, preferred_element_type=jnp.float32)
    weight_total, kernel_total = sum_weights(weight_part, kernel_part)

    dattended = jnp.einsum(
        "rd,ad->ra", dhidden, out_weight, preferred_element_type=jnp.float32
    ).astype(jnp.bfloat16)
    dout_heads = split_heads(dattended)
    deltas = jnp.einsum("rhe,rhe->hr", dout_heads, attended, preferred_element_type=jnp.float32)

    probs = jnp.where(visible, jnp.exp(scores - log_sums[..., None]), 0.0)
    dvalue_heads = jnp.einsum(
        "hqk,qhd->khd", probs.astype(jnp.bfloat16), dout_heads, preferred_element_type=jnp.float32
    )
    dprobs = jnp.einsum("qhd,khd->hqk", dout_heads, value_heads, preferred_element_type=jnp.float32)
    dscores = (probs * (dprobs - deltas[..., None])).astype(jnp.bfloat16)
    dquery = (
        jnp.einsum("hqk,khd->qhd", dscores, key_heads, preferred_element_type=jnp.float32)
        * score_scale
    )
    dkey_heads = (
        jnp.einsum("hqk,qhd->khd", dscores, query_heads, preferred_element_type=jnp.float32)
        * score_scale
    )
    window_rows = window.shape[0]
    dkv = jnp.concatenate(
        [dkey_heads.reshape(window_rows, ATT), dvalue_heads.reshape(window_rows, ATT)], axis=1
    )
    dkv_total = dkv[context * row_count:]
    for slot, offset in enumerate(offsets):
        part = dkv[slot * row_count:(slot + 1) * row_count].astype(jnp.bfloat16)
        dkv_total = dkv_total + from_behind(part, "blk", -offset).astype(jnp.float32)

    query_grad = dquery.reshape(row_count, ATT).astype(jnp.bfloat16)[None]
    key_grad = dkv_total[:, :ATT].astype(jnp.bfloat16)[None]
    value_grad = dkv_total[:, ATT:].astype(jnp.bfloat16)[None]
    return (out_frames, query_grad, key_grad, value_grad, weight_total, kernel_total)


def solution(mesh):
    return jax.shard_map(
        per_device,
        mesh=mesh,
        in_specs=(
            P("dp", "blk", None),
            P("dp", "blk", None),
            P("dp", "blk", None),
            P(),
            P(),
            P("dp", "blk", None),
        ),
        out_specs=(
            P("dp", "blk", None),
            P("dp", "blk", None),
            P("dp", "blk", None),
            P("dp", "blk", None),
            P(),
            P(),
        ),
        check_vma=False,
    )
```

```python
import functools
import math

import jax
import jax.numpy as jnp
from jax import lax
from jax.experimental import pallas as pl
from jax.experimental.pallas import tpu as pltpu
from jax.sharding import PartitionSpec as P

ATT_HEADS = 8
HEAD_DIM = 64
CTX_MAX = 3
ATT = 512


NEGATIVE = -1e30
MESH_ID = pl.DeviceIdType.MESH


def reduce_bits(dp_size, blk_size):
    if dp_size == 4 and blk_size == 128:
        return [("dp", 1), ("dp", 2), ("blk", 16), ("blk", 2), ("blk", 32),
                ("blk", 4), ("blk", 64), ("blk", 8), ("blk", 1)]
    bits = []
    for axis, size in (("dp", dp_size), ("blk", blk_size)):
        m = 1
        while m < size:
            bits.append((axis, m))
            m *= 2
    return bits


def allreduce_kernel(bits, n_halve, x_ref, o_ref, *scratch):
    halves = scratch[:n_halve]
    doubles = scratch[n_halve:len(bits)]
    acc, send_sem, recv_sem = scratch[len(bits):]
    me = {"dp": lax.axis_index("dp"), "blk": lax.axis_index("blk")}

    def partner(axis, m):
        bit = (me[axis] // m) % 2
        peer = me[axis] + m - 2 * m * bit
        ids = (peer, me["blk"]) if axis == "dp" else (me["dp"], peer)
        return bit, ids

    barrier = pltpu.get_barrier_semaphore()
    for axis, m in bits:
        pl.semaphore_signal(barrier, 1, device_id=partner(axis, m)[1], device_id_type=MESH_ID)
    pl.semaphore_wait(barrier, len(bits))

    offset = 0
    length = o_ref.shape[0]
    plan = []
    for step in range(n_halve):
        axis, m = bits[step]
        half = length // 2
        bit, ids = partner(axis, m)
        keep = offset + bit * half
        give = offset + (1 - bit) * half
        source = x_ref if step == 0 else acc
        copy = pltpu.make_async_remote_copy(
            src_ref=source.at[pl.ds(give, half)], dst_ref=halves[step],
            send_sem=send_sem.at[step], recv_sem=recv_sem.at[step],
            device_id=ids, device_id_type=MESH_ID)
        copy.start()
        copy.wait()
        acc[pl.ds(keep, half)] = source[pl.ds(keep, half)] + halves[step][...]
        plan.append((ids, keep, half))
        offset, length = keep, half
    for slot, (axis, m) in enumerate(bits[n_halve:]):
        step = n_halve + slot
        bit, ids = partner(axis, m)
        copy = pltpu.make_async_remote_copy(
            src_ref=acc.at[pl.ds(offset, length)], dst_ref=doubles[slot],
            send_sem=send_sem.at[step], recv_sem=recv_sem.at[step],
            device_id=ids, device_id_type=MESH_ID)
        copy.start()
        copy.wait()
        acc[pl.ds(offset, length)] = acc[pl.ds(offset, length)] + doubles[slot][...]
    o_ref[pl.ds(offset, length)] = acc[pl.ds(offset, length)]
    for back, (ids, keep, half) in enumerate(reversed(plan)):
        step = len(bits) + back
        copy = pltpu.make_async_remote_copy(
            src_ref=o_ref.at[pl.ds(keep, half)], dst_ref=o_ref.at[pl.ds(keep, half)],
            send_sem=send_sem.at[step], recv_sem=recv_sem.at[step],
            device_id=ids, device_id_type=MESH_ID)
        copy.start()
        copy.wait()


def allreduce(x, dp_size, blk_size, n_halve_max=5):
    bits = reduce_bits(dp_size, blk_size)
    rows = x.shape[0]
    n_halve = 0
    while n_halve < min(n_halve_max, len(bits)) and rows % (2 ** (n_halve + 1)) == 0:
        n_halve += 1
    lengths = [rows // 2 ** (s + 1) for s in range(n_halve)]
    final = rows // 2 ** n_halve
    tile = x.shape[1:]
    scratch = [pltpu.VMEM((n,) + tile, x.dtype) for n in lengths]
    scratch += [pltpu.VMEM((final,) + tile, x.dtype) for _ in bits[n_halve:]]
    steps = len(bits) + n_halve
    scratch += [pltpu.VMEM(x.shape, x.dtype), pltpu.SemaphoreType.DMA((steps,)), pltpu.SemaphoreType.DMA((steps,))]
    return pl.pallas_call(
        functools.partial(allreduce_kernel, bits, n_halve),
        out_shape=jax.ShapeDtypeStruct(x.shape, x.dtype),
        in_specs=[pl.BlockSpec(memory_space=pltpu.VMEM)],
        out_specs=pl.BlockSpec(memory_space=pltpu.VMEM),
        scratch_shapes=scratch,
        compiler_params=pltpu.CompilerParams(collective_id=0, has_side_effects=True),
    )(x)


def from_behind(block, axis, distance):
    devices = range(lax.axis_size(axis))
    route = [(i - distance, i) for i in devices if i - distance in devices]
    return lax.ppermute(block, axis, route)


def split_heads(matrix):
    return matrix.reshape(matrix.shape[0], ATT_HEADS, HEAD_DIM)


def depthwise(extended, conv_kernel, row_count, ahead):
    tap_count = conv_kernel.shape[0]
    total = None
    for tap_index in range(tap_count):
        first_row = tap_index if ahead else tap_count - 1 - tap_index
        term = conv_kernel[tap_index] * extended[first_row:first_row + row_count]
        total = term if total is None else total + term
    return total


def sum_weights(weight_part, kernel_part):
    width = weight_part.shape[1]
    rows = weight_part.shape[0] + kernel_part.shape[0]
    padded = -(-rows // 32) * 32
    packed = jnp.concatenate(
        [weight_part, kernel_part, jnp.zeros((padded - rows, width), jnp.float32)], axis=0
    )
    total = allreduce(
        packed.reshape(padded, 8, width // 8),
        lax.axis_size("dp"),
        lax.axis_size("blk"),
    ).reshape(padded, width)
    return total[: weight_part.shape[0]], total[weight_part.shape[0] : rows]


def per_device(queries, key_in, value_in, out_weight, conv_kernel, cotangent):
    cycle_count = lax.axis_size("blk")
    device = lax.axis_index("blk")
    row_count = queries.shape[1]
    context = min(CTX_MAX, cycle_count // 4)
    left_span = context * row_count
    score_scale = 1.0 / math.sqrt(HEAD_DIM)
    edge_rows = conv_kernel.shape[0] - 1
    row_ids = jnp.arange(row_count, dtype=jnp.int32)
    query_heads = split_heads(queries[0])
    own_tile = jnp.concatenate([key_in[0], value_in[0]], axis=1)
    own_pos = device * row_count + row_ids

    offsets = list(range(context, 0, -1))
    window = jnp.concatenate(
        [from_behind(own_tile, "blk", offset) for offset in offsets] + [own_tile], axis=0
    )
    key_pos = jnp.concatenate([(device - offset) * row_count + row_ids for offset in offsets] + [own_pos])
    distance = own_pos[:, None] - key_pos[None, :]
    visible = ((distance >= 0) & (distance < left_span) & (key_pos[None, :] >= 0))[None]
    key_heads = split_heads(window[:, :ATT])
    value_heads = split_heads(window[:, ATT:])

    scores = (
        jnp.einsum("qhd,khd->hqk", query_heads, key_heads, preferred_element_type=jnp.float32)
        * score_scale
    )
    scores = jnp.where(visible, scores, NEGATIVE)
    row_max = jnp.max(scores, axis=-1)
    weights = jnp.where(visible, jnp.exp(scores - row_max[..., None]), 0.0)
    row_sum = jnp.sum(weights, axis=-1)
    weighted = jnp.einsum(
        "hqk,khd->qhd", weights.astype(jnp.bfloat16), value_heads, preferred_element_type=jnp.float32
    )
    attended = (weighted / jnp.transpose(row_sum)[:, :, None]).astype(jnp.bfloat16)
    log_sums = row_max + jnp.log(row_sum)
    flat = attended.reshape(row_count, ATT)

    hidden = jnp.dot(flat, out_weight, preferred_element_type=jnp.float32).astype(jnp.bfloat16)
    before = from_behind(hidden[-edge_rows:], "blk", 1)
    following = from_behind(
        jnp.concatenate([hidden[:edge_rows], cotangent[0][:edge_rows]], axis=1), "blk", -1
    )
    width = hidden.shape[1]
    extended = jnp.concatenate([before, hidden, following[:, :width]], axis=0).astype(jnp.float32)
    mixed_all = depthwise(extended, conv_kernel, row_count + edge_rows, False)
    sigma_all = jax.nn.sigmoid(mixed_all)
    upstream = jnp.concatenate([cotangent[0], following[:, width:]], axis=0).astype(jnp.float32)
    dmixed_all = upstream * sigma_all * (1.0 + mixed_all * (1.0 - sigma_all))
    out_frames = (mixed_all[:row_count] * sigma_all[:row_count]).astype(jnp.bfloat16)[None]
    dmixed = dmixed_all[:row_count]
    dhidden = depthwise(dmixed_all, conv_kernel, row_count, True).astype(jnp.bfloat16)

    windows = jnp.stack(
        [extended[edge_rows - tap:edge_rows - tap + row_count] for tap in range(edge_rows + 1)]
    )
    kernel_part = jnp.sum(windows * dmixed[None], axis=1)
    weight_part = jnp.einsum("ra,rd->ad", flat, dhidden, preferred_element_type=jnp.float32)
    weight_total, kernel_total = sum_weights(weight_part, kernel_part)

    dattended = jnp.einsum(
        "rd,ad->ra", dhidden, out_weight, preferred_element_type=jnp.float32
    ).astype(jnp.bfloat16)
    dout_heads = split_heads(dattended)
    deltas = jnp.einsum("rhe,rhe->hr", dout_heads, attended, preferred_element_type=jnp.float32)

    probs = jnp.where(visible, jnp.exp(scores - log_sums[..., None]), 0.0)
    dvalue_heads = jnp.einsum(
        "hqk,qhd->khd", probs.astype(jnp.bfloat16), dout_heads, preferred_element_type=jnp.float32
    )
    dprobs = jnp.einsum("qhd,khd->hqk", dout_heads, value_heads, preferred_element_type=jnp.float32)
    dscores = (probs * (dprobs - deltas[..., None])).astype(jnp.bfloat16)
    dquery = (
        jnp.einsum("hqk,khd->qhd", dscores, key_heads, preferred_element_type=jnp.float32)
        * score_scale
    )
    dkey_heads = (
        jnp.einsum("hqk,qhd->khd", dscores, query_heads, preferred_element_type=jnp.float32)
        * score_scale
    )
    window_rows = window.shape[0]
    dkv = jnp.concatenate(
        [dkey_heads.reshape(window_rows, ATT), dvalue_heads.reshape(window_rows, ATT)], axis=1
    )
    dkv_total = dkv[context * row_count:]
    for slot, offset in enumerate(offsets):
        part = dkv[slot * row_count:(slot + 1) * row_count].astype(jnp.bfloat16)
        dkv_total = dkv_total + from_behind(part, "blk", -offset).astype(jnp.float32)

    query_grad = dquery.reshape(row_count, ATT).astype(jnp.bfloat16)[None]
    key_grad = dkv_total[:, :ATT].astype(jnp.bfloat16)[None]
    value_grad = dkv_total[:, ATT:].astype(jnp.bfloat16)[None]
    return (out_frames, query_grad, key_grad, value_grad, weight_total, kernel_total)


def solution(mesh):
    return jax.shard_map(
        per_device,
        mesh=mesh,
        in_specs=(
            P("dp", "blk", None),
            P("dp", "blk", None),
            P("dp", "blk", None),
            P(),
            P(),
            P("dp", "blk", None),
        ),
        out_specs=(
            P("dp", "blk", None),
            P("dp", "blk", None),
            P("dp", "blk", None),
            P("dp", "blk", None),
            P(),
            P(),
        ),
        check_vma=False,
    )
```

```python
import functools
import math

import jax
import jax.numpy as jnp
from jax import lax
from jax.experimental import pallas as pl
from jax.experimental.pallas import tpu as pltpu
from jax.sharding import PartitionSpec as P

ATT_HEADS = 8
HEAD_DIM = 64
CTX_MAX = 3
ATT = 512


NEGATIVE = -1e30
MESH_ID = pl.DeviceIdType.MESH


def reduce_bits(dp_size, blk_size):
    if dp_size == 4 and blk_size == 128:
        return [("dp", 1), ("dp", 2), ("blk", 16), ("blk", 2), ("blk", 32),
                ("blk", 4), ("blk", 64), ("blk", 8), ("blk", 1)]
    bits = []
    for axis, size in (("dp", dp_size), ("blk", blk_size)):
        m = 1
        while m < size:
            bits.append((axis, m))
            m *= 2
    return bits


def allreduce_kernel(bits, n_halve, x_ref, o_ref, *scratch):
    halves = scratch[:n_halve]
    doubles = scratch[n_halve:len(bits)]
    acc, send_sem, recv_sem = scratch[len(bits):]
    me = {"dp": lax.axis_index("dp"), "blk": lax.axis_index("blk")}

    def partner(axis, m):
        bit = (me[axis] // m) % 2
        peer = me[axis] + m - 2 * m * bit
        ids = (peer, me["blk"]) if axis == "dp" else (me["dp"], peer)
        return bit, ids

    barrier = pltpu.get_barrier_semaphore()
    for axis, m in bits:
        pl.semaphore_signal(barrier, 1, device_id=partner(axis, m)[1], device_id_type=MESH_ID)
    pl.semaphore_wait(barrier, len(bits))

    offset = 0
    length = o_ref.shape[0]
    plan = []
    for step in range(n_halve):
        axis, m = bits[step]
        half = length // 2
        bit, ids = partner(axis, m)
        keep = offset + bit * half
        give = offset + (1 - bit) * half
        source = x_ref if step == 0 else acc
        copy = pltpu.make_async_remote_copy(
            src_ref=source.at[pl.ds(give, half)], dst_ref=halves[step],
            send_sem=send_sem.at[step], recv_sem=recv_sem.at[step],
            device_id=ids, device_id_type=MESH_ID)
        copy.start()
        copy.wait()
        acc[pl.ds(keep, half)] = source[pl.ds(keep, half)] + halves[step][...]
        plan.append((ids, keep, half))
        offset, length = keep, half
    for slot, (axis, m) in enumerate(bits[n_halve:]):
        step = n_halve + slot
        bit, ids = partner(axis, m)
        copy = pltpu.make_async_remote_copy(
            src_ref=acc.at[pl.ds(offset, length)], dst_ref=doubles[slot],
            send_sem=send_sem.at[step], recv_sem=recv_sem.at[step],
            device_id=ids, device_id_type=MESH_ID)
        copy.start()
        copy.wait()
        acc[pl.ds(offset, length)] = acc[pl.ds(offset, length)] + doubles[slot][...]
    o_ref[pl.ds(offset, length)] = acc[pl.ds(offset, length)]
    for back, (ids, keep, half) in enumerate(reversed(plan)):
        step = len(bits) + back
        copy = pltpu.make_async_remote_copy(
            src_ref=o_ref.at[pl.ds(keep, half)], dst_ref=o_ref.at[pl.ds(keep, half)],
            send_sem=send_sem.at[step], recv_sem=recv_sem.at[step],
            device_id=ids, device_id_type=MESH_ID)
        copy.start()
        copy.wait()


def allreduce(x, dp_size, blk_size, n_halve_max=5):
    bits = reduce_bits(dp_size, blk_size)
    rows = x.shape[0]
    n_halve = 0
    while n_halve < min(n_halve_max, len(bits)) and rows % (2 ** (n_halve + 1)) == 0:
        n_halve += 1
    lengths = [rows // 2 ** (s + 1) for s in range(n_halve)]
    final = rows // 2 ** n_halve
    tile = x.shape[1:]
    scratch = [pltpu.VMEM((n,) + tile, x.dtype) for n in lengths]
    scratch += [pltpu.VMEM((final,) + tile, x.dtype) for _ in bits[n_halve:]]
    steps = len(bits) + n_halve
    scratch += [pltpu.VMEM(x.shape, x.dtype), pltpu.SemaphoreType.DMA((steps,)), pltpu.SemaphoreType.DMA((steps,))]
    return pl.pallas_call(
        functools.partial(allreduce_kernel, bits, n_halve),
        out_shape=jax.ShapeDtypeStruct(x.shape, x.dtype),
        in_specs=[pl.BlockSpec(memory_space=pltpu.VMEM)],
        out_specs=pl.BlockSpec(memory_space=pltpu.VMEM),
        scratch_shapes=scratch,
        compiler_params=pltpu.CompilerParams(collective_id=0, has_side_effects=True),
    )(x)


def from_behind(block, axis, distance):
    devices = range(lax.axis_size(axis))
    route = [(i - distance, i) for i in devices if i - distance in devices]
    return lax.ppermute(block, axis, route)


def split_heads(matrix):
    return matrix.reshape(matrix.shape[0], ATT_HEADS, HEAD_DIM)


def depthwise(extended, conv_kernel, row_count, ahead):
    tap_count = conv_kernel.shape[0]
    total = None
    for tap_index in range(tap_count):
        first_row = tap_index if ahead else tap_count - 1 - tap_index
        term = conv_kernel[tap_index] * extended[first_row:first_row + row_count]
        total = term if total is None else total + term
    return total


def kernel_taps_body(tap_count, dmixed_ref, extended_ref, out_ref):
    rows = dmixed_ref.shape[0]
    first = tap_count - 1
    grads = dmixed_ref[...]
    for tap in range(tap_count):
        window = extended_ref[pl.ds(first - tap, rows), :]
        out_ref[pl.ds(tap, 1), :] = jnp.sum(grads * window, axis=0, keepdims=True)
    out_ref[pl.ds(tap_count, out_ref.shape[0] - tap_count), :] = jnp.zeros(
        (out_ref.shape[0] - tap_count, out_ref.shape[1]), jnp.float32
    )


def kernel_taps(dmixed, extended, tap_count):
    padded = -(-tap_count // 8) * 8
    return pl.pallas_call(
        functools.partial(kernel_taps_body, tap_count),
        out_shape=jax.ShapeDtypeStruct((padded, dmixed.shape[1]), jnp.float32),
        in_specs=[pl.BlockSpec(memory_space=pltpu.VMEM)] * 2,
        out_specs=pl.BlockSpec(memory_space=pltpu.VMEM),
    )(dmixed, extended)


def sum_weights(weight_part, kernel_part, kernel_rows):
    width = weight_part.shape[1]
    rows = weight_part.shape[0] + kernel_part.shape[0]
    packed = jnp.concatenate([weight_part, kernel_part], axis=0)
    total = allreduce(
        packed.reshape(rows, 8, width // 8), lax.axis_size("dp"), lax.axis_size("blk")
    ).reshape(rows, width)
    start = weight_part.shape[0]
    return total[:start], total[start:start + kernel_rows]


def per_device(queries, key_in, value_in, out_weight, conv_kernel, cotangent):
    cycle_count = lax.axis_size("blk")
    device = lax.axis_index("blk")
    row_count = queries.shape[1]
    context = min(CTX_MAX, cycle_count // 4)
    left_span = context * row_count
    score_scale = 1.0 / math.sqrt(HEAD_DIM)
    edge_rows = conv_kernel.shape[0] - 1
    row_ids = jnp.arange(row_count, dtype=jnp.int32)
    query_heads = split_heads(queries[0])
    own_tile = jnp.concatenate([key_in[0], value_in[0]], axis=1)
    own_pos = device * row_count + row_ids

    offsets = list(range(context, 0, -1))
    window = jnp.concatenate(
        [from_behind(own_tile, "blk", offset) for offset in offsets] + [own_tile], axis=0
    )
    key_pos = jnp.concatenate([(device - offset) * row_count + row_ids for offset in offsets] + [own_pos])
    distance = own_pos[:, None] - key_pos[None, :]
    visible = ((distance >= 0) & (distance < left_span) & (key_pos[None, :] >= 0))[None]
    key_heads = split_heads(window[:, :ATT])
    value_heads = split_heads(window[:, ATT:])

    scores = (
        jnp.einsum("qhd,khd->hqk", query_heads, key_heads, preferred_element_type=jnp.float32)
        * score_scale
    )
    scores = jnp.where(visible, scores, NEGATIVE)
    row_max = jnp.max(scores, axis=-1)
    weights = jnp.where(visible, jnp.exp(scores - row_max[..., None]), 0.0)
    row_sum = jnp.sum(weights, axis=-1)
    weighted = jnp.einsum(
        "hqk,khd->qhd", weights.astype(jnp.bfloat16), value_heads, preferred_element_type=jnp.float32
    )
    attended = (weighted / jnp.transpose(row_sum)[:, :, None]).astype(jnp.bfloat16)
    log_sums = row_max + jnp.log(row_sum)
    flat = attended.reshape(row_count, ATT)

    hidden = jnp.dot(flat, out_weight, preferred_element_type=jnp.float32).astype(jnp.bfloat16)
    before = from_behind(hidden[-edge_rows:], "blk", 1)
    following = from_behind(
        jnp.concatenate([hidden[:edge_rows], cotangent[0][:edge_rows]], axis=1), "blk", -1
    )
    width = hidden.shape[1]
    extended = jnp.concatenate([before, hidden, following[:, :width]], axis=0).astype(jnp.float32)
    mixed_all = depthwise(extended, conv_kernel, row_count + edge_rows, False)
    sigma_all = jax.nn.sigmoid(mixed_all)
    upstream = jnp.concatenate([cotangent[0], following[:, width:]], axis=0).astype(jnp.float32)
    dmixed_all = upstream * sigma_all * (1.0 + mixed_all * (1.0 - sigma_all))
    out_frames = (mixed_all[:row_count] * sigma_all[:row_count]).astype(jnp.bfloat16)[None]
    dmixed = dmixed_all[:row_count]
    dhidden = depthwise(dmixed_all, conv_kernel, row_count, True).astype(jnp.bfloat16)

    kernel_part = kernel_taps(dmixed, extended[: row_count + edge_rows], edge_rows + 1)
    weight_part = jnp.einsum("ra,rd->ad", flat, dhidden, preferred_element_type=jnp.float32)
    weight_total, kernel_total = sum_weights(weight_part, kernel_part, edge_rows + 1)

    dattended = jnp.einsum(
        "rd,ad->ra", dhidden, out_weight, preferred_element_type=jnp.float32
    ).astype(jnp.bfloat16)
    dout_heads = split_heads(dattended)
    deltas = jnp.einsum("rhe,rhe->hr", dout_heads, attended, preferred_element_type=jnp.float32)

    probs = jnp.where(visible, jnp.exp(scores - log_sums[..., None]), 0.0)
    dvalue_heads = jnp.einsum(
        "hqk,qhd->khd", probs.astype(jnp.bfloat16), dout_heads, preferred_element_type=jnp.float32
    )
    dprobs = jnp.einsum("qhd,khd->hqk", dout_heads, value_heads, preferred_element_type=jnp.float32)
    dscores = (probs * (dprobs - deltas[..., None])).astype(jnp.bfloat16)
    dquery = (
        jnp.einsum("hqk,khd->qhd", dscores, key_heads, preferred_element_type=jnp.float32)
        * score_scale
    )
    dkey_heads = (
        jnp.einsum("hqk,qhd->khd", dscores, query_heads, preferred_element_type=jnp.float32)
        * score_scale
    )
    window_rows = window.shape[0]
    dkv = jnp.concatenate(
        [dkey_heads.reshape(window_rows, ATT), dvalue_heads.reshape(window_rows, ATT)], axis=1
    )
    dkv_total = dkv[context * row_count:]
    for slot, offset in enumerate(offsets):
        part = dkv[slot * row_count:(slot + 1) * row_count].astype(jnp.bfloat16)
        dkv_total = dkv_total + from_behind(part, "blk", -offset).astype(jnp.float32)

    query_grad = dquery.reshape(row_count, ATT).astype(jnp.bfloat16)[None]
    key_grad = dkv_total[:, :ATT].astype(jnp.bfloat16)[None]
    value_grad = dkv_total[:, ATT:].astype(jnp.bfloat16)[None]
    return (out_frames, query_grad, key_grad, value_grad, weight_total, kernel_total)


def solution(mesh):
    return jax.shard_map(
        per_device,
        mesh=mesh,
        in_specs=(
            P("dp", "blk", None),
            P("dp", "blk", None),
            P("dp", "blk", None),
            P(),
            P(),
            P("dp", "blk", None),
        ),
        out_specs=(
            P("dp", "blk", None),
            P("dp", "blk", None),
            P("dp", "blk", None),
            P("dp", "blk", None),
            P(),
            P(),
        ),
        check_vma=False,
    )
```

```python
import functools
import math

import jax
import jax.numpy as jnp
from jax import lax
from jax.experimental import pallas as pl
from jax.experimental.pallas import tpu as pltpu
from jax.sharding import PartitionSpec as P

ATT_HEADS = 8
HEAD_DIM = 64
CTX_MAX = 3
ATT = 512


NEGATIVE = -1e30
MESH_ID = pl.DeviceIdType.MESH


def reduce_bits(dp_size, blk_size):
    if dp_size == 4 and blk_size == 128:
        core0 = [("dp", 1), ("dp", 2), ("blk", 16), ("blk", 2), ("blk", 32),
                 ("blk", 4), ("blk", 64), ("blk", 8), ("blk", 1)]
        core1 = [("dp", 1), ("blk", 16), ("dp", 2), ("blk", 32), ("blk", 2),
                 ("blk", 64), ("blk", 4), ("blk", 1), ("blk", 8)]
        return list(zip(core0, core1))
    bits = []
    for axis, size in (("dp", dp_size), ("blk", blk_size)):
        m = 1
        while m < size:
            bits.append(((axis, m), (axis, m)))
            m *= 2
    return bits


def allreduce_kernel(bits, n_halve, x_ref, o_ref, *scratch):
    halves = scratch[:n_halve]
    doubles = scratch[n_halve:len(bits)]
    acc, send_sem, recv_sem = scratch[len(bits):]
    me = {"dp": lax.axis_index("dp"), "blk": lax.axis_index("blk")}

    core = me["dp"] % 2

    def one_partner(axis, m):
        bit = (me[axis] // m) % 2
        peer = me[axis] + m - 2 * m * bit
        ids = (peer, me["blk"]) if axis == "dp" else (me["dp"], peer)
        return bit, ids

    def partner(specs):
        bit0, ids0 = one_partner(*specs[0])
        bit1, ids1 = one_partner(*specs[1])
        bit = bit0 + (bit1 - bit0) * core
        ids = tuple(a + (b - a) * core for a, b in zip(ids0, ids1))
        return bit, ids

    barrier = pltpu.get_barrier_semaphore()
    for specs in bits:
        pl.semaphore_signal(barrier, 1, device_id=partner(specs)[1], device_id_type=MESH_ID)
    pl.semaphore_wait(barrier, len(bits))

    offset = 0
    length = o_ref.shape[0]
    plan = []
    for step in range(n_halve):
        half = length // 2
        bit, ids = partner(bits[step])
        keep = offset + bit * half
        give = offset + (1 - bit) * half
        source = x_ref if step == 0 else acc
        copy = pltpu.make_async_remote_copy(
            src_ref=source.at[pl.ds(give, half)], dst_ref=halves[step],
            send_sem=send_sem.at[step], recv_sem=recv_sem.at[step],
            device_id=ids, device_id_type=MESH_ID)
        copy.start()
        copy.wait()
        acc[pl.ds(keep, half)] = source[pl.ds(keep, half)] + halves[step][...]
        plan.append((ids, keep, half))
        offset, length = keep, half
    for slot, specs in enumerate(bits[n_halve:]):
        step = n_halve + slot
        bit, ids = partner(specs)
        copy = pltpu.make_async_remote_copy(
            src_ref=acc.at[pl.ds(offset, length)], dst_ref=doubles[slot],
            send_sem=send_sem.at[step], recv_sem=recv_sem.at[step],
            device_id=ids, device_id_type=MESH_ID)
        copy.start()
        copy.wait()
        acc[pl.ds(offset, length)] = acc[pl.ds(offset, length)] + doubles[slot][...]
    o_ref[pl.ds(offset, length)] = acc[pl.ds(offset, length)]
    for back, (ids, keep, half) in enumerate(reversed(plan)):
        step = len(bits) + back
        copy = pltpu.make_async_remote_copy(
            src_ref=o_ref.at[pl.ds(keep, half)], dst_ref=o_ref.at[pl.ds(keep, half)],
            send_sem=send_sem.at[step], recv_sem=recv_sem.at[step],
            device_id=ids, device_id_type=MESH_ID)
        copy.start()
        copy.wait()


def allreduce(x, dp_size, blk_size, n_halve_max=5):
    bits = reduce_bits(dp_size, blk_size)
    rows = x.shape[0]
    n_halve = 0
    while n_halve < min(n_halve_max, len(bits)) and rows % (2 ** (n_halve + 1)) == 0:
        n_halve += 1
    lengths = [rows // 2 ** (s + 1) for s in range(n_halve)]
    final = rows // 2 ** n_halve
    tile = x.shape[1:]
    scratch = [pltpu.VMEM((n,) + tile, x.dtype) for n in lengths]
    scratch += [pltpu.VMEM((final,) + tile, x.dtype) for _ in bits[n_halve:]]
    steps = len(bits) + n_halve
    scratch += [pltpu.VMEM(x.shape, x.dtype), pltpu.SemaphoreType.DMA((steps,)), pltpu.SemaphoreType.DMA((steps,))]
    return pl.pallas_call(
        functools.partial(allreduce_kernel, bits, n_halve),
        out_shape=jax.ShapeDtypeStruct(x.shape, x.dtype),
        in_specs=[pl.BlockSpec(memory_space=pltpu.VMEM)],
        out_specs=pl.BlockSpec(memory_space=pltpu.VMEM),
        scratch_shapes=scratch,
        compiler_params=pltpu.CompilerParams(collective_id=0, has_side_effects=True),
    )(x)


def from_behind(block, axis, distance):
    devices = range(lax.axis_size(axis))
    route = [(i - distance, i) for i in devices if i - distance in devices]
    return lax.ppermute(block, axis, route)


def split_heads(matrix):
    return matrix.reshape(matrix.shape[0], ATT_HEADS, HEAD_DIM)


def depthwise(extended, conv_kernel, row_count, ahead):
    tap_count = conv_kernel.shape[0]
    total = None
    for tap_index in range(tap_count):
        first_row = tap_index if ahead else tap_count - 1 - tap_index
        term = conv_kernel[tap_index] * extended[first_row:first_row + row_count]
        total = term if total is None else total + term
    return total


def kernel_taps_body(tap_count, dmixed_ref, extended_ref, out_ref):
    rows = dmixed_ref.shape[0]
    first = tap_count - 1
    grads = dmixed_ref[...]
    for tap in range(tap_count):
        window = extended_ref[pl.ds(first - tap, rows), :]
        out_ref[pl.ds(tap, 1), :] = jnp.sum(grads * window, axis=0, keepdims=True)
    out_ref[pl.ds(tap_count, out_ref.shape[0] - tap_count), :] = jnp.zeros(
        (out_ref.shape[0] - tap_count, out_ref.shape[1]), jnp.float32
    )


def kernel_taps(dmixed, extended, tap_count):
    padded = -(-tap_count // 8) * 8
    return pl.pallas_call(
        functools.partial(kernel_taps_body, tap_count),
        out_shape=jax.ShapeDtypeStruct((padded, dmixed.shape[1]), jnp.float32),
        in_specs=[pl.BlockSpec(memory_space=pltpu.VMEM)] * 2,
        out_specs=pl.BlockSpec(memory_space=pltpu.VMEM),
    )(dmixed, extended)


def sum_weights(weight_part, kernel_part, kernel_rows):
    width = weight_part.shape[1]
    rows = weight_part.shape[0] + kernel_part.shape[0]
    packed = jnp.concatenate([weight_part, kernel_part], axis=0)
    total = allreduce(
        packed.reshape(rows, 8, width // 8), lax.axis_size("dp"), lax.axis_size("blk")
    ).reshape(rows, width)
    start = weight_part.shape[0]
    return total[:start], total[start:start + kernel_rows]


def per_device(queries, key_in, value_in, out_weight, conv_kernel, cotangent):
    cycle_count = lax.axis_size("blk")
    device = lax.axis_index("blk")
    row_count = queries.shape[1]
    context = min(CTX_MAX, cycle_count // 4)
    left_span = context * row_count
    score_scale = 1.0 / math.sqrt(HEAD_DIM)
    edge_rows = conv_kernel.shape[0] - 1
    row_ids = jnp.arange(row_count, dtype=jnp.int32)
    query_heads = split_heads(queries[0])
    own_tile = jnp.concatenate([key_in[0], value_in[0]], axis=1)
    own_pos = device * row_count + row_ids

    offsets = list(range(context, 0, -1))
    window = jnp.concatenate(
        [from_behind(own_tile, "blk", offset) for offset in offsets] + [own_tile], axis=0
    )
    key_pos = jnp.concatenate([(device - offset) * row_count + row_ids for offset in offsets] + [own_pos])
    distance = own_pos[:, None] - key_pos[None, :]
    visible = ((distance >= 0) & (distance < left_span) & (key_pos[None, :] >= 0))[None]
    key_heads = split_heads(window[:, :ATT])
    value_heads = split_heads(window[:, ATT:])

    scores = (
        jnp.einsum("qhd,khd->hqk", query_heads, key_heads, preferred_element_type=jnp.float32)
        * score_scale
    )
    scores = jnp.where(visible, scores, NEGATIVE)
    row_max = jnp.max(scores, axis=-1)
    weights = jnp.where(visible, jnp.exp(scores - row_max[..., None]), 0.0)
    row_sum = jnp.sum(weights, axis=-1)
    weighted = jnp.einsum(
        "hqk,khd->qhd", weights.astype(jnp.bfloat16), value_heads, preferred_element_type=jnp.float32
    )
    attended = (weighted / jnp.transpose(row_sum)[:, :, None]).astype(jnp.bfloat16)
    log_sums = row_max + jnp.log(row_sum)
    flat = attended.reshape(row_count, ATT)

    hidden = jnp.dot(flat, out_weight, preferred_element_type=jnp.float32).astype(jnp.bfloat16)
    before = from_behind(hidden[-edge_rows:], "blk", 1)
    following = from_behind(
        jnp.concatenate([hidden[:edge_rows], cotangent[0][:edge_rows]], axis=1), "blk", -1
    )
    width = hidden.shape[1]
    extended = jnp.concatenate([before, hidden, following[:, :width]], axis=0).astype(jnp.float32)
    mixed_all = depthwise(extended, conv_kernel, row_count + edge_rows, False)
    sigma_all = jax.nn.sigmoid(mixed_all)
    upstream = jnp.concatenate([cotangent[0], following[:, width:]], axis=0).astype(jnp.float32)
    dmixed_all = upstream * sigma_all * (1.0 + mixed_all * (1.0 - sigma_all))
    out_frames = (mixed_all[:row_count] * sigma_all[:row_count]).astype(jnp.bfloat16)[None]
    dmixed = dmixed_all[:row_count]
    dhidden = depthwise(dmixed_all, conv_kernel, row_count, True).astype(jnp.bfloat16)

    kernel_part = kernel_taps(dmixed, extended[: row_count + edge_rows], edge_rows + 1)
    weight_part = jnp.einsum("ra,rd->ad", flat, dhidden, preferred_element_type=jnp.float32)
    weight_total, kernel_total = sum_weights(weight_part, kernel_part, edge_rows + 1)

    dattended = jnp.einsum(
        "rd,ad->ra", dhidden, out_weight, preferred_element_type=jnp.float32
    ).astype(jnp.bfloat16)
    dout_heads = split_heads(dattended)
    deltas = jnp.einsum("rhe,rhe->hr", dout_heads, attended, preferred_element_type=jnp.float32)

    probs = jnp.where(visible, jnp.exp(scores - log_sums[..., None]), 0.0)
    dvalue_heads = jnp.einsum(
        "hqk,qhd->khd", probs.astype(jnp.bfloat16), dout_heads, preferred_element_type=jnp.float32
    )
    dprobs = jnp.einsum("qhd,khd->hqk", dout_heads, value_heads, preferred_element_type=jnp.float32)
    dscores = (probs * (dprobs - deltas[..., None])).astype(jnp.bfloat16)
    dquery = (
        jnp.einsum("hqk,khd->qhd", dscores, key_heads, preferred_element_type=jnp.float32)
        * score_scale
    )
    dkey_heads = (
        jnp.einsum("hqk,qhd->khd", dscores, query_heads, preferred_element_type=jnp.float32)
        * score_scale
    )
    window_rows = window.shape[0]
    dkv = jnp.concatenate(
        [dkey_heads.reshape(window_rows, ATT), dvalue_heads.reshape(window_rows, ATT)], axis=1
    )
    dkv_total = dkv[context * row_count:]
    for slot, offset in enumerate(offsets):
        part = dkv[slot * row_count:(slot + 1) * row_count].astype(jnp.bfloat16)
        dkv_total = dkv_total + from_behind(part, "blk", -offset).astype(jnp.float32)

    query_grad = dquery.reshape(row_count, ATT).astype(jnp.bfloat16)[None]
    key_grad = dkv_total[:, :ATT].astype(jnp.bfloat16)[None]
    value_grad = dkv_total[:, ATT:].astype(jnp.bfloat16)[None]
    return (out_frames, query_grad, key_grad, value_grad, weight_total, kernel_total)


def solution(mesh):
    return jax.shard_map(
        per_device,
        mesh=mesh,
        in_specs=(
            P("dp", "blk", None),
            P("dp", "blk", None),
            P("dp", "blk", None),
            P(),
            P(),
            P("dp", "blk", None),
        ),
        out_specs=(
            P("dp", "blk", None),
            P("dp", "blk", None),
            P("dp", "blk", None),
            P("dp", "blk", None),
            P(),
            P(),
        ),
        check_vma=False,
    )
```

```python
import functools
import math

import jax
import jax.numpy as jnp
from jax import lax
from jax.experimental import pallas as pl
from jax.experimental.pallas import tpu as pltpu
from jax.sharding import PartitionSpec as P

ATT_HEADS = 8
HEAD_DIM = 64
CTX_MAX = 3
ATT = 512


NEGATIVE = -1e30
MESH_ID = pl.DeviceIdType.MESH


def reduce_bits(dp_size, blk_size):
    if dp_size == 4 and blk_size == 128:
        core0 = [("dp", 1), ("dp", 2), ("blk", 16), ("blk", 2), ("blk", 32),
                 ("blk", 4), ("blk", 64), ("blk", 8), ("blk", 1)]
        core1 = [("dp", 1), ("blk", 16), ("dp", 2), ("blk", 32), ("blk", 2),
                 ("blk", 64), ("blk", 4), ("blk", 1), ("blk", 8)]
        return list(zip(core0, core1))
    bits = []
    for axis, size in (("dp", dp_size), ("blk", blk_size)):
        m = 1
        while m < size:
            bits.append(((axis, m), (axis, m)))
            m *= 2
    return bits


def allreduce_kernel(bits, splits, n_arrays, *refs):
    x_refs = refs[:n_arrays]
    o_refs = refs[n_arrays:2 * n_arrays]
    scratch = refs[2 * n_arrays:]
    n_halve = len(splits)
    halves = [scratch[s * n_arrays:(s + 1) * n_arrays] for s in range(n_halve)]
    base = n_halve * n_arrays
    n_double = len(bits) - n_halve
    doubles = [scratch[base + t * n_arrays:base + (t + 1) * n_arrays] for t in range(n_double)]
    base += n_double * n_arrays
    accs = scratch[base:base + n_arrays]
    send_sem, recv_sem = scratch[base + n_arrays:]
    me = {"dp": lax.axis_index("dp"), "blk": lax.axis_index("blk")}
    core = me["dp"] % 2

    def one_partner(axis, m):
        bit = (me[axis] // m) % 2
        peer = me[axis] + m - 2 * m * bit
        ids = (peer, me["blk"]) if axis == "dp" else (me["dp"], peer)
        return bit, ids

    def partner(specs):
        bit0, ids0 = one_partner(*specs[0])
        bit1, ids1 = one_partner(*specs[1])
        bit = bit0 + (bit1 - bit0) * core
        ids = tuple(a + (b - a) * core for a, b in zip(ids0, ids1))
        return bit, ids

    def window(ref, region):
        r0, rl, c0, cl = region
        return ref.at[pl.ds(pl.multiple_of(r0, 8), rl), pl.ds(pl.multiple_of(c0, 128), cl)]

    def exchange(step, ids, sources, targets, regions):
        copies = []
        for i in range(n_arrays):
            copy = pltpu.make_async_remote_copy(
                src_ref=window(sources[i], regions[i]), dst_ref=targets[i],
                send_sem=send_sem.at[step, i], recv_sem=recv_sem.at[step, i],
                device_id=ids, device_id_type=MESH_ID)
            copy.start()
            copies.append(copy)
        for copy in copies:
            copy.wait()

    barrier = pltpu.get_barrier_semaphore()
    for specs in bits:
        pl.semaphore_signal(barrier, 1, device_id=partner(specs)[1], device_id_type=MESH_ID)
    pl.semaphore_wait(barrier, len(bits))

    regions = [(0, x.shape[0], 0, x.shape[1]) for x in x_refs]
    plan = []
    for step, dim in enumerate(splits):
        bit, ids = partner(bits[step])
        keeps, gives = [], []
        for r0, rl, c0, cl in regions:
            if dim == 0:
                half = rl // 2
                keeps.append((r0 + bit * half, half, c0, cl))
                gives.append((r0 + (1 - bit) * half, half, c0, cl))
            else:
                half = cl // 2
                keeps.append((r0, rl, c0 + bit * half, half))
                gives.append((r0, rl, c0 + (1 - bit) * half, half))
        sources = x_refs if step == 0 else accs
        exchange(step, ids, sources, [h.at[...] for h in halves[step]], gives)
        for i in range(n_arrays):
            window(accs[i], keeps[i])[...] = window(sources[i], keeps[i])[...] + halves[step][i][...]
        plan.append((ids, keeps))
        regions = keeps
    for slot in range(n_double):
        step = n_halve + slot
        bit, ids = partner(bits[step])
        exchange(step, ids, accs, [d.at[...] for d in doubles[slot]], regions)
        for i in range(n_arrays):
            window(accs[i], regions[i])[...] = window(accs[i], regions[i])[...] + doubles[slot][i][...]
    for i in range(n_arrays):
        window(o_refs[i], regions[i])[...] = window(accs[i], regions[i])[...]
    for back, (ids, keeps) in enumerate(reversed(plan)):
        step = len(bits) + back
        exchange(step, ids, o_refs, [window(o, k) for o, k in zip(o_refs, keeps)], keeps)


def allreduce(arrays, dp_size, blk_size, n_halve_max=5):
    bits = reduce_bits(dp_size, blk_size)
    limit = min(n_halve_max, len(bits))
    splits = []
    cols = arrays[0].shape[1]
    rows = [a.shape[0] for a in arrays]
    while len(splits) < limit and cols % 256 == 0:
        splits.append(1)
        cols //= 2
    while len(splits) < limit and all(r % 16 == 0 for r in rows):
        splits.append(0)
        rows = [r // 2 for r in rows]
    scratch = []
    shapes = [a.shape for a in arrays]
    for dim in splits:
        shapes = [(s[0] // 2, s[1]) if dim == 0 else (s[0], s[1] // 2) for s in shapes]
        scratch += [pltpu.VMEM(s, jnp.float32) for s in shapes]
    for _ in bits[len(splits):]:
        scratch += [pltpu.VMEM(s, jnp.float32) for s in shapes]
    scratch += [pltpu.VMEM(a.shape, jnp.float32) for a in arrays]
    steps = len(bits) + len(splits)
    scratch += [pltpu.SemaphoreType.DMA((steps, len(arrays))), pltpu.SemaphoreType.DMA((steps, len(arrays)))]
    return pl.pallas_call(
        functools.partial(allreduce_kernel, bits, splits, len(arrays)),
        out_shape=[jax.ShapeDtypeStruct(a.shape, jnp.float32) for a in arrays],
        in_specs=[pl.BlockSpec(memory_space=pltpu.VMEM)] * len(arrays),
        out_specs=[pl.BlockSpec(memory_space=pltpu.VMEM)] * len(arrays),
        scratch_shapes=scratch,
        compiler_params=pltpu.CompilerParams(collective_id=0, has_side_effects=True),
    )(*arrays)


def from_behind(block, axis, distance):
    devices = range(lax.axis_size(axis))
    route = [(i - distance, i) for i in devices if i - distance in devices]
    return lax.ppermute(block, axis, route)


def split_heads(matrix):
    return matrix.reshape(matrix.shape[0], ATT_HEADS, HEAD_DIM)


def depthwise(extended, conv_kernel, row_count, ahead):
    tap_count = conv_kernel.shape[0]
    total = None
    for tap_index in range(tap_count):
        first_row = tap_index if ahead else tap_count - 1 - tap_index
        term = conv_kernel[tap_index] * extended[first_row:first_row + row_count]
        total = term if total is None else total + term
    return total


def kernel_taps_body(tap_count, dmixed_ref, extended_ref, out_ref):
    rows = dmixed_ref.shape[0]
    first = tap_count - 1
    grads = dmixed_ref[...]
    for tap in range(tap_count):
        window = extended_ref[pl.ds(first - tap, rows), :]
        out_ref[pl.ds(tap, 1), :] = jnp.sum(grads * window, axis=0, keepdims=True)
    out_ref[pl.ds(tap_count, out_ref.shape[0] - tap_count), :] = jnp.zeros(
        (out_ref.shape[0] - tap_count, out_ref.shape[1]), jnp.float32
    )


def kernel_taps(dmixed, extended, tap_count):
    padded = -(-tap_count // 8) * 8
    return pl.pallas_call(
        functools.partial(kernel_taps_body, tap_count),
        out_shape=jax.ShapeDtypeStruct((padded, dmixed.shape[1]), jnp.float32),
        in_specs=[pl.BlockSpec(memory_space=pltpu.VMEM)] * 2,
        out_specs=pl.BlockSpec(memory_space=pltpu.VMEM),
    )(dmixed, extended)


def sum_weights(weight_part, kernel_part, kernel_rows):
    weight_total, kernel_total = allreduce(
        [weight_part, kernel_part], lax.axis_size("dp"), lax.axis_size("blk")
    )
    return weight_total, kernel_total[:kernel_rows]


def per_device(queries, key_in, value_in, out_weight, conv_kernel, cotangent):
    cycle_count = lax.axis_size("blk")
    device = lax.axis_index("blk")
    row_count = queries.shape[1]
    context = min(CTX_MAX, cycle_count // 4)
    left_span = context * row_count
    score_scale = 1.0 / math.sqrt(HEAD_DIM)
    edge_rows = conv_kernel.shape[0] - 1
    row_ids = jnp.arange(row_count, dtype=jnp.int32)
    query_heads = split_heads(queries[0])
    own_tile = jnp.concatenate([key_in[0], value_in[0]], axis=1)
    own_pos = device * row_count + row_ids

    offsets = list(range(context, 0, -1))
    window = jnp.concatenate(
        [from_behind(own_tile, "blk", offset) for offset in offsets] + [own_tile], axis=0
    )
    key_pos = jnp.concatenate([(device - offset) * row_count + row_ids for offset in offsets] + [own_pos])
    distance = own_pos[:, None] - key_pos[None, :]
    visible = ((distance >= 0) & (distance < left_span) & (key_pos[None, :] >= 0))[None]
    key_heads = split_heads(window[:, :ATT])
    value_heads = split_heads(window[:, ATT:])

    scores = (
        jnp.einsum("qhd,khd->hqk", query_heads, key_heads, preferred_element_type=jnp.float32)
        * score_scale
    )
    scores = jnp.where(visible, scores, NEGATIVE)
    row_max = jnp.max(scores, axis=-1)
    weights = jnp.where(visible, jnp.exp(scores - row_max[..., None]), 0.0)
    row_sum = jnp.sum(weights, axis=-1)
    weighted = jnp.einsum(
        "hqk,khd->qhd", weights.astype(jnp.bfloat16), value_heads, preferred_element_type=jnp.float32
    )
    attended = (weighted / jnp.transpose(row_sum)[:, :, None]).astype(jnp.bfloat16)
    log_sums = row_max + jnp.log(row_sum)
    flat = attended.reshape(row_count, ATT)

    hidden = jnp.dot(flat, out_weight, preferred_element_type=jnp.float32).astype(jnp.bfloat16)
    before = from_behind(hidden[-edge_rows:], "blk", 1)
    following = from_behind(
        jnp.concatenate([hidden[:edge_rows], cotangent[0][:edge_rows]], axis=1), "blk", -1
    )
    width = hidden.shape[1]
    extended = jnp.concatenate([before, hidden, following[:, :width]], axis=0).astype(jnp.float32)
    mixed_all = depthwise(extended, conv_kernel, row_count + edge_rows, False)
    sigma_all = jax.nn.sigmoid(mixed_all)
    upstream = jnp.concatenate([cotangent[0], following[:, width:]], axis=0).astype(jnp.float32)
    dmixed_all = upstream * sigma_all * (1.0 + mixed_all * (1.0 - sigma_all))
    out_frames = (mixed_all[:row_count] * sigma_all[:row_count]).astype(jnp.bfloat16)[None]
    dmixed = dmixed_all[:row_count]
    dhidden = depthwise(dmixed_all, conv_kernel, row_count, True).astype(jnp.bfloat16)

    kernel_part = kernel_taps(dmixed, extended[: row_count + edge_rows], edge_rows + 1)
    weight_part = jnp.einsum("ra,rd->ad", flat, dhidden, preferred_element_type=jnp.float32)
    weight_total, kernel_total = sum_weights(weight_part, kernel_part, edge_rows + 1)

    dattended = jnp.einsum(
        "rd,ad->ra", dhidden, out_weight, preferred_element_type=jnp.float32
    ).astype(jnp.bfloat16)
    dout_heads = split_heads(dattended)
    deltas = jnp.einsum("rhe,rhe->hr", dout_heads, attended, preferred_element_type=jnp.float32)

    probs = jnp.where(visible, jnp.exp(scores - log_sums[..., None]), 0.0)
    dvalue_heads = jnp.einsum(
        "hqk,qhd->khd", probs.astype(jnp.bfloat16), dout_heads, preferred_element_type=jnp.float32
    )
    dprobs = jnp.einsum("qhd,khd->hqk", dout_heads, value_heads, preferred_element_type=jnp.float32)
    dscores = (probs * (dprobs - deltas[..., None])).astype(jnp.bfloat16)
    dquery = (
        jnp.einsum("hqk,khd->qhd", dscores, key_heads, preferred_element_type=jnp.float32)
        * score_scale
    )
    dkey_heads = (
        jnp.einsum("hqk,qhd->khd", dscores, query_heads, preferred_element_type=jnp.float32)
        * score_scale
    )
    window_rows = window.shape[0]
    dkv = jnp.concatenate(
        [dkey_heads.reshape(window_rows, ATT), dvalue_heads.reshape(window_rows, ATT)], axis=1
    )
    dkv_total = dkv[context * row_count:]
    for slot, offset in enumerate(offsets):
        part = dkv[slot * row_count:(slot + 1) * row_count].astype(jnp.bfloat16)
        dkv_total = dkv_total + from_behind(part, "blk", -offset).astype(jnp.float32)

    query_grad = dquery.reshape(row_count, ATT).astype(jnp.bfloat16)[None]
    key_grad = dkv_total[:, :ATT].astype(jnp.bfloat16)[None]
    value_grad = dkv_total[:, ATT:].astype(jnp.bfloat16)[None]
    return (out_frames, query_grad, key_grad, value_grad, weight_total, kernel_total)


def solution(mesh):
    return jax.shard_map(
        per_device,
        mesh=mesh,
        in_specs=(
            P("dp", "blk", None),
            P("dp", "blk", None),
            P("dp", "blk", None),
            P(),
            P(),
            P("dp", "blk", None),
        ),
        out_specs=(
            P("dp", "blk", None),
            P("dp", "blk", None),
            P("dp", "blk", None),
            P("dp", "blk", None),
            P(),
            P(),
        ),
        check_vma=False,
    )
```

```python
import functools
import math

import jax
import jax.numpy as jnp
from jax import lax
from jax.experimental import pallas as pl
from jax.experimental.pallas import tpu as pltpu
from jax.sharding import PartitionSpec as P

ATT_HEADS = 8
HEAD_DIM = 64
CTX_MAX = 3
ATT = 512


NEGATIVE = -1e30
MESH_ID = pl.DeviceIdType.MESH
FIRST_PIECES = 4


def reduce_bits(dp_size, blk_size):
    if dp_size == 4 and blk_size == 128:
        core0 = [("dp", 1), ("dp", 2), ("blk", 16), ("blk", 2), ("blk", 32),
                 ("blk", 4), ("blk", 64), ("blk", 8), ("blk", 1)]
        core1 = [("dp", 1), ("blk", 16), ("dp", 2), ("blk", 32), ("blk", 2),
                 ("blk", 64), ("blk", 4), ("blk", 1), ("blk", 8)]
        return list(zip(core0, core1))
    bits = []
    for axis, size in (("dp", dp_size), ("blk", blk_size)):
        m = 1
        while m < size:
            bits.append(((axis, m), (axis, m)))
            m *= 2
    return bits


def allreduce_kernel(bits, splits, n_arrays, *refs):
    x_refs = refs[:n_arrays]
    o_refs = refs[n_arrays:2 * n_arrays]
    scratch = refs[2 * n_arrays:]
    n_halve = len(splits)
    halves = [scratch[s * n_arrays:(s + 1) * n_arrays] for s in range(n_halve)]
    base = n_halve * n_arrays
    n_double = len(bits) - n_halve
    doubles = [scratch[base + t * n_arrays:base + (t + 1) * n_arrays] for t in range(n_double)]
    base += n_double * n_arrays
    accs = scratch[base:base + n_arrays]
    send_sem, recv_sem = scratch[base + n_arrays:]
    me = {"dp": lax.axis_index("dp"), "blk": lax.axis_index("blk")}
    core = me["dp"] % 2

    def one_partner(axis, m):
        bit = (me[axis] // m) % 2
        peer = me[axis] + m - 2 * m * bit
        ids = (peer, me["blk"]) if axis == "dp" else (me["dp"], peer)
        return bit, ids

    def partner(specs):
        bit0, ids0 = one_partner(*specs[0])
        bit1, ids1 = one_partner(*specs[1])
        bit = bit0 + (bit1 - bit0) * core
        ids = tuple(a + (b - a) * core for a, b in zip(ids0, ids1))
        return bit, ids

    def window(ref, region):
        r0, rl, c0, cl = region
        return ref.at[pl.ds(pl.multiple_of(r0, 8), rl), pl.ds(pl.multiple_of(c0, 128), cl)]

    def exchange(step, ids, sources, targets, regions, pieces=1):
        copies = []
        for i in range(n_arrays):
            r0, rl, c0, cl = regions[i]
            part = rl // pieces
            for p in range(pieces):
                piece = (r0 + p * part, part, c0, cl)
                copy = pltpu.make_async_remote_copy(
                    src_ref=window(sources[i], piece),
                    dst_ref=targets[i].at[pl.ds(p * part, part), :],
                    send_sem=send_sem.at[step, i, p], recv_sem=recv_sem.at[step, i, p],
                    device_id=ids, device_id_type=MESH_ID)
                copy.start()
                copies.append(copy)
        for copy in copies:
            copy.wait()

    barrier = pltpu.get_barrier_semaphore()
    for specs in bits:
        pl.semaphore_signal(barrier, 1, device_id=partner(specs)[1], device_id_type=MESH_ID)
    pl.semaphore_wait(barrier, len(bits))

    regions = [(0, x.shape[0], 0, x.shape[1]) for x in x_refs]
    plan = []
    for step, dim in enumerate(splits):
        bit, ids = partner(bits[step])
        keeps, gives = [], []
        for r0, rl, c0, cl in regions:
            if dim == 0:
                half = rl // 2
                keeps.append((r0 + bit * half, half, c0, cl))
                gives.append((r0 + (1 - bit) * half, half, c0, cl))
            else:
                half = cl // 2
                keeps.append((r0, rl, c0 + bit * half, half))
                gives.append((r0, rl, c0 + (1 - bit) * half, half))
        sources = x_refs if step == 0 else accs
        exchange(step, ids, sources, [h.at[...] for h in halves[step]], gives, FIRST_PIECES if step == 0 else 1)
        for i in range(n_arrays):
            window(accs[i], keeps[i])[...] = window(sources[i], keeps[i])[...] + halves[step][i][...]
        plan.append((ids, keeps))
        regions = keeps
    for slot in range(n_double):
        step = n_halve + slot
        bit, ids = partner(bits[step])
        exchange(step, ids, accs, [d.at[...] for d in doubles[slot]], regions)
        for i in range(n_arrays):
            window(accs[i], regions[i])[...] = window(accs[i], regions[i])[...] + doubles[slot][i][...]
    for i in range(n_arrays):
        window(o_refs[i], regions[i])[...] = window(accs[i], regions[i])[...]
    for back, (ids, keeps) in enumerate(reversed(plan)):
        step = len(bits) + back
        targets = [window(o, (k[0], k[1], k[2], k[3])) for o, k in zip(o_refs, keeps)]
        pieces = FIRST_PIECES if back == len(plan) - 1 else 1
        exchange(step, ids, o_refs, targets, keeps, pieces)


def allreduce(arrays, dp_size, blk_size, n_halve_max=5):
    bits = reduce_bits(dp_size, blk_size)
    limit = min(n_halve_max, len(bits))
    splits = []
    cols = arrays[0].shape[1]
    rows = [a.shape[0] for a in arrays]
    while len(splits) < limit and cols % 256 == 0:
        splits.append(1)
        cols //= 2
    while len(splits) < limit and all(r % 16 == 0 for r in rows):
        splits.append(0)
        rows = [r // 2 for r in rows]
    scratch = []
    shapes = [a.shape for a in arrays]
    for dim in splits:
        shapes = [(s[0] // 2, s[1]) if dim == 0 else (s[0], s[1] // 2) for s in shapes]
        scratch += [pltpu.VMEM(s, jnp.float32) for s in shapes]
    for _ in bits[len(splits):]:
        scratch += [pltpu.VMEM(s, jnp.float32) for s in shapes]
    scratch += [pltpu.VMEM(a.shape, jnp.float32) for a in arrays]
    steps = len(bits) + len(splits)
    sems = (steps, len(arrays), FIRST_PIECES)
    scratch += [pltpu.SemaphoreType.DMA(sems), pltpu.SemaphoreType.DMA(sems)]
    return pl.pallas_call(
        functools.partial(allreduce_kernel, bits, splits, len(arrays)),
        out_shape=[jax.ShapeDtypeStruct(a.shape, jnp.float32) for a in arrays],
        in_specs=[pl.BlockSpec(memory_space=pltpu.VMEM)] * len(arrays),
        out_specs=[pl.BlockSpec(memory_space=pltpu.VMEM)] * len(arrays),
        scratch_shapes=scratch,
        compiler_params=pltpu.CompilerParams(collective_id=0, has_side_effects=True),
    )(*arrays)


def from_behind(block, axis, distance):
    devices = range(lax.axis_size(axis))
    route = [(i - distance, i) for i in devices if i - distance in devices]
    return lax.ppermute(block, axis, route)


def split_heads(matrix):
    return matrix.reshape(matrix.shape[0], ATT_HEADS, HEAD_DIM)


def depthwise(extended, conv_kernel, row_count, ahead):
    tap_count = conv_kernel.shape[0]
    total = None
    for tap_index in range(tap_count):
        first_row = tap_index if ahead else tap_count - 1 - tap_index
        term = conv_kernel[tap_index] * extended[first_row:first_row + row_count]
        total = term if total is None else total + term
    return total


def kernel_taps_body(tap_count, dmixed_ref, extended_ref, out_ref):
    rows = dmixed_ref.shape[0]
    first = tap_count - 1
    grads = dmixed_ref[...]
    for tap in range(tap_count):
        window = extended_ref[pl.ds(first - tap, rows), :]
        out_ref[pl.ds(tap, 1), :] = jnp.sum(grads * window, axis=0, keepdims=True)
    out_ref[pl.ds(tap_count, out_ref.shape[0] - tap_count), :] = jnp.zeros(
        (out_ref.shape[0] - tap_count, out_ref.shape[1]), jnp.float32
    )


def kernel_taps(dmixed, extended, tap_count):
    padded = -(-tap_count // 8) * 8
    return pl.pallas_call(
        functools.partial(kernel_taps_body, tap_count),
        out_shape=jax.ShapeDtypeStruct((padded, dmixed.shape[1]), jnp.float32),
        in_specs=[pl.BlockSpec(memory_space=pltpu.VMEM)] * 2,
        out_specs=pl.BlockSpec(memory_space=pltpu.VMEM),
    )(dmixed, extended)


def sum_weights(weight_part, kernel_part, kernel_rows):
    weight_total, kernel_total = allreduce(
        [weight_part, kernel_part], lax.axis_size("dp"), lax.axis_size("blk")
    )
    return weight_total, kernel_total[:kernel_rows]


def per_device(queries, key_in, value_in, out_weight, conv_kernel, cotangent):
    cycle_count = lax.axis_size("blk")
    device = lax.axis_index("blk")
    row_count = queries.shape[1]
    context = min(CTX_MAX, cycle_count // 4)
    left_span = context * row_count
    score_scale = 1.0 / math.sqrt(HEAD_DIM)
    edge_rows = conv_kernel.shape[0] - 1
    row_ids = jnp.arange(row_count, dtype=jnp.int32)
    query_heads = split_heads(queries[0])
    own_tile = jnp.concatenate([key_in[0], value_in[0]], axis=1)
    own_pos = device * row_count + row_ids

    offsets = list(range(context, 0, -1))
    window = jnp.concatenate(
        [from_behind(own_tile, "blk", offset) for offset in offsets] + [own_tile], axis=0
    )
    key_pos = jnp.concatenate([(device - offset) * row_count + row_ids for offset in offsets] + [own_pos])
    distance = own_pos[:, None] - key_pos[None, :]
    visible = ((distance >= 0) & (distance < left_span) & (key_pos[None, :] >= 0))[None]
    key_heads = split_heads(window[:, :ATT])
    value_heads = split_heads(window[:, ATT:])

    scores = (
        jnp.einsum("qhd,khd->hqk", query_heads, key_heads, preferred_element_type=jnp.float32)
        * score_scale
    )
    scores = jnp.where(visible, scores, NEGATIVE)
    row_max = jnp.max(scores, axis=-1)
    weights = jnp.where(visible, jnp.exp(scores - row_max[..., None]), 0.0)
    row_sum = jnp.sum(weights, axis=-1)
    weighted = jnp.einsum(
        "hqk,khd->qhd", weights.astype(jnp.bfloat16), value_heads, preferred_element_type=jnp.float32
    )
    attended = (weighted / jnp.transpose(row_sum)[:, :, None]).astype(jnp.bfloat16)
    log_sums = row_max + jnp.log(row_sum)
    flat = attended.reshape(row_count, ATT)

    hidden = jnp.dot(flat, out_weight, preferred_element_type=jnp.float32).astype(jnp.bfloat16)
    before = from_behind(hidden[-edge_rows:], "blk", 1)
    following = from_behind(
        jnp.concatenate([hidden[:edge_rows], cotangent[0][:edge_rows]], axis=1), "blk", -1
    )
    width = hidden.shape[1]
    extended = jnp.concatenate([before, hidden, following[:, :width]], axis=0).astype(jnp.float32)
    mixed_all = depthwise(extended, conv_kernel, row_count + edge_rows, False)
    sigma_all = jax.nn.sigmoid(mixed_all)
    upstream = jnp.concatenate([cotangent[0], following[:, width:]], axis=0).astype(jnp.float32)
    dmixed_all = upstream * sigma_all * (1.0 + mixed_all * (1.0 - sigma_all))
    out_frames = (mixed_all[:row_count] * sigma_all[:row_count]).astype(jnp.bfloat16)[None]
    dmixed = dmixed_all[:row_count]
    dhidden = depthwise(dmixed_all, conv_kernel, row_count, True).astype(jnp.bfloat16)

    kernel_part = kernel_taps(dmixed, extended[: row_count + edge_rows], edge_rows + 1)
    weight_part = jnp.einsum("ra,rd->ad", flat, dhidden, preferred_element_type=jnp.float32)
    weight_total, kernel_total = sum_weights(weight_part, kernel_part, edge_rows + 1)

    dattended = jnp.einsum(
        "rd,ad->ra", dhidden, out_weight, preferred_element_type=jnp.float32
    ).astype(jnp.bfloat16)
    dout_heads = split_heads(dattended)
    deltas = jnp.einsum("rhe,rhe->hr", dout_heads, attended, preferred_element_type=jnp.float32)

    probs = jnp.where(visible, jnp.exp(scores - log_sums[..., None]), 0.0)
    dvalue_heads = jnp.einsum(
        "hqk,qhd->khd", probs.astype(jnp.bfloat16), dout_heads, preferred_element_type=jnp.float32
    )
    dprobs = jnp.einsum("qhd,khd->hqk", dout_heads, value_heads, preferred_element_type=jnp.float32)
    dscores = (probs * (dprobs - deltas[..., None])).astype(jnp.bfloat16)
    dquery = (
        jnp.einsum("hqk,khd->qhd", dscores, key_heads, preferred_element_type=jnp.float32)
        * score_scale
    )
    dkey_heads = (
        jnp.einsum("hqk,qhd->khd", dscores, query_heads, preferred_element_type=jnp.float32)
        * score_scale
    )
    window_rows = window.shape[0]
    dkv = jnp.concatenate(
        [dkey_heads.reshape(window_rows, ATT), dvalue_heads.reshape(window_rows, ATT)], axis=1
    )
    dkv_total = dkv[context * row_count:]
    for slot, offset in enumerate(offsets):
        part = dkv[slot * row_count:(slot + 1) * row_count].astype(jnp.bfloat16)
        dkv_total = dkv_total + from_behind(part, "blk", -offset).astype(jnp.float32)

    query_grad = dquery.reshape(row_count, ATT).astype(jnp.bfloat16)[None]
    key_grad = dkv_total[:, :ATT].astype(jnp.bfloat16)[None]
    value_grad = dkv_total[:, ATT:].astype(jnp.bfloat16)[None]
    return (out_frames, query_grad, key_grad, value_grad, weight_total, kernel_total)


def solution(mesh):
    return jax.shard_map(
        per_device,
        mesh=mesh,
        in_specs=(
            P("dp", "blk", None),
            P("dp", "blk", None),
            P("dp", "blk", None),
            P(),
            P(),
            P("dp", "blk", None),
        ),
        out_specs=(
            P("dp", "blk", None),
            P("dp", "blk", None),
            P("dp", "blk", None),
            P("dp", "blk", None),
            P(),
            P(),
        ),
        check_vma=False,
    )
```

```python
import functools
import math

import jax
import jax.numpy as jnp
from jax import lax
from jax.experimental import pallas as pl
from jax.experimental.pallas import tpu as pltpu
from jax.sharding import PartitionSpec as P

ATT_HEADS = 8
HEAD_DIM = 64
CTX_MAX = 3
ATT = 512


NEGATIVE = -1e30
MESH_ID = pl.DeviceIdType.MESH


def reduce_bits(dp_size, blk_size):
    if dp_size == 4 and blk_size == 128:
        core0 = [("dp", 1), ("dp", 2), ("blk", 16), ("blk", 2), ("blk", 32),
                 ("blk", 4), ("blk", 64), ("blk", 8), ("blk", 1)]
        core1 = [("dp", 1), ("blk", 16), ("dp", 2), ("blk", 32), ("blk", 2),
                 ("blk", 64), ("blk", 4), ("blk", 1), ("blk", 8)]
        return list(zip(core0, core1))
    bits = []
    for axis, size in (("dp", dp_size), ("blk", blk_size)):
        m = 1
        while m < size:
            bits.append(((axis, m), (axis, m)))
            m *= 2
    return bits


def allreduce_kernel(bits, splits, n_arrays, *refs):
    x_refs = refs[:n_arrays]
    o_refs = refs[n_arrays:2 * n_arrays]
    scratch = refs[2 * n_arrays:]
    n_halve = len(splits)
    halves = [scratch[s * n_arrays:(s + 1) * n_arrays] for s in range(n_halve)]
    base = n_halve * n_arrays
    n_double = len(bits) - n_halve
    doubles = [scratch[base + t * n_arrays:base + (t + 1) * n_arrays] for t in range(n_double)]
    base += n_double * n_arrays
    accs = scratch[base:base + n_arrays]
    send_sem, recv_sem = scratch[base + n_arrays:]
    me = {"dp": lax.axis_index("dp"), "blk": lax.axis_index("blk")}
    core = me["dp"] % 2

    def one_partner(axis, m):
        bit = (me[axis] // m) % 2
        peer = me[axis] + m - 2 * m * bit
        ids = (peer, me["blk"]) if axis == "dp" else (me["dp"], peer)
        return bit, ids

    def partner(specs):
        bit0, ids0 = one_partner(*specs[0])
        bit1, ids1 = one_partner(*specs[1])
        bit = bit0 + (bit1 - bit0) * core
        ids = tuple(a + (b - a) * core for a, b in zip(ids0, ids1))
        return bit, ids

    def window(ref, region):
        r0, rl, c0, cl = region
        return ref.at[pl.ds(pl.multiple_of(r0, 8), rl), pl.ds(pl.multiple_of(c0, 128), cl)]

    def exchange(step, ids, sources, targets, regions):
        copies = []
        for i in range(n_arrays):
            copy = pltpu.make_async_remote_copy(
                src_ref=window(sources[i], regions[i]), dst_ref=targets[i],
                send_sem=send_sem.at[step, i], recv_sem=recv_sem.at[step, i],
                device_id=ids, device_id_type=MESH_ID)
            copy.start()
            copies.append(copy)
        for copy in copies:
            copy.wait()

    barrier = pltpu.get_barrier_semaphore()
    for specs in bits:
        pl.semaphore_signal(barrier, 1, device_id=partner(specs)[1], device_id_type=MESH_ID)
    pl.semaphore_wait(barrier, len(bits))

    regions = [(0, x.shape[0], 0, x.shape[1]) for x in x_refs]
    plan = []
    for step, dim in enumerate(splits):
        bit, ids = partner(bits[step])
        keeps, gives = [], []
        for r0, rl, c0, cl in regions:
            if dim == 0:
                half = rl // 2
                keeps.append((r0 + bit * half, half, c0, cl))
                gives.append((r0 + (1 - bit) * half, half, c0, cl))
            else:
                half = cl // 2
                keeps.append((r0, rl, c0 + bit * half, half))
                gives.append((r0, rl, c0 + (1 - bit) * half, half))
        sources = x_refs if step == 0 else accs
        exchange(step, ids, sources, [h.at[...] for h in halves[step]], gives)
        for i in range(n_arrays):
            window(accs[i], keeps[i])[...] = window(sources[i], keeps[i])[...] + halves[step][i][...]
        plan.append((ids, keeps))
        regions = keeps
    for slot in range(n_double):
        step = n_halve + slot
        bit, ids = partner(bits[step])
        exchange(step, ids, accs, [d.at[...] for d in doubles[slot]], regions)
        for i in range(n_arrays):
            window(accs[i], regions[i])[...] = window(accs[i], regions[i])[...] + doubles[slot][i][...]
    for i in range(n_arrays):
        window(o_refs[i], regions[i])[...] = window(accs[i], regions[i])[...]
    for back, (ids, keeps) in enumerate(reversed(plan)):
        step = len(bits) + back
        exchange(step, ids, o_refs, [window(o, k) for o, k in zip(o_refs, keeps)], keeps)


def allreduce(arrays, dp_size, blk_size, n_halve_max=5):
    bits = reduce_bits(dp_size, blk_size)
    limit = min(n_halve_max, len(bits))
    splits = []
    cols = arrays[0].shape[1]
    rows = [a.shape[0] for a in arrays]
    while len(splits) < limit and cols % 256 == 0:
        splits.append(1)
        cols //= 2
    while len(splits) < limit and all(r % 16 == 0 for r in rows):
        splits.append(0)
        rows = [r // 2 for r in rows]
    scratch = []
    shapes = [a.shape for a in arrays]
    for dim in splits:
        shapes = [(s[0] // 2, s[1]) if dim == 0 else (s[0], s[1] // 2) for s in shapes]
        scratch += [pltpu.VMEM(s, jnp.float32) for s in shapes]
    for _ in bits[len(splits):]:
        scratch += [pltpu.VMEM(s, jnp.float32) for s in shapes]
    scratch += [pltpu.VMEM(a.shape, jnp.float32) for a in arrays]
    steps = len(bits) + len(splits)
    scratch += [pltpu.SemaphoreType.DMA((steps, len(arrays))), pltpu.SemaphoreType.DMA((steps, len(arrays)))]
    return pl.pallas_call(
        functools.partial(allreduce_kernel, bits, splits, len(arrays)),
        out_shape=[jax.ShapeDtypeStruct(a.shape, jnp.float32) for a in arrays],
        in_specs=[pl.BlockSpec(memory_space=pltpu.VMEM)] * len(arrays),
        out_specs=[pl.BlockSpec(memory_space=pltpu.VMEM)] * len(arrays),
        scratch_shapes=scratch,
        compiler_params=pltpu.CompilerParams(collective_id=0, has_side_effects=True),
    )(*arrays)


def from_behind(block, axis, distance):
    devices = range(lax.axis_size(axis))
    route = [(i - distance, i) for i in devices if i - distance in devices]
    return lax.ppermute(block, axis, route)


def split_heads(matrix):
    return matrix.reshape(matrix.shape[0], ATT_HEADS, HEAD_DIM)


def depthwise(extended, conv_kernel, row_count, ahead):
    tap_count = conv_kernel.shape[0]
    total = None
    for tap_index in range(tap_count):
        first_row = tap_index if ahead else tap_count - 1 - tap_index
        term = conv_kernel[tap_index] * extended[first_row:first_row + row_count]
        total = term if total is None else total + term
    return total


def kernel_taps_body(tap_count, dmixed_ref, extended_ref, out_ref):
    rows = dmixed_ref.shape[0]
    first = tap_count - 1
    grads = dmixed_ref[...]
    shifted = []
    for shift in range(8):
        span = (first - shift) // 8 * 8 + rows if shift <= first else 0
        shifted.append(extended_ref[pl.ds(shift, span), :] if span else None)
    for tap in range(tap_count):
        block, shift = divmod(first - tap, 8)
        window = shifted[shift][block * 8:block * 8 + rows]
        out_ref[pl.ds(tap, 1), :] = jnp.sum(grads * window, axis=0, keepdims=True)
    out_ref[pl.ds(tap_count, out_ref.shape[0] - tap_count), :] = jnp.zeros(
        (out_ref.shape[0] - tap_count, out_ref.shape[1]), jnp.float32
    )


def kernel_taps(dmixed, extended, tap_count):
    padded = -(-tap_count // 8) * 8
    return pl.pallas_call(
        functools.partial(kernel_taps_body, tap_count),
        out_shape=jax.ShapeDtypeStruct((padded, dmixed.shape[1]), jnp.float32),
        in_specs=[pl.BlockSpec(memory_space=pltpu.VMEM)] * 2,
        out_specs=pl.BlockSpec(memory_space=pltpu.VMEM),
    )(dmixed, extended)


def sum_weights(weight_part, kernel_part, kernel_rows):
    weight_total, kernel_total = allreduce(
        [weight_part, kernel_part], lax.axis_size("dp"), lax.axis_size("blk")
    )
    return weight_total, kernel_total[:kernel_rows]


def per_device(queries, key_in, value_in, out_weight, conv_kernel, cotangent):
    cycle_count = lax.axis_size("blk")
    device = lax.axis_index("blk")
    row_count = queries.shape[1]
    context = min(CTX_MAX, cycle_count // 4)
    left_span = context * row_count
    score_scale = 1.0 / math.sqrt(HEAD_DIM)
    edge_rows = conv_kernel.shape[0] - 1
    row_ids = jnp.arange(row_count, dtype=jnp.int32)
    query_heads = split_heads(queries[0])
    own_tile = jnp.concatenate([key_in[0], value_in[0]], axis=1)
    own_pos = device * row_count + row_ids

    offsets = list(range(context, 0, -1))
    window = jnp.concatenate(
        [from_behind(own_tile, "blk", offset) for offset in offsets] + [own_tile], axis=0
    )
    key_pos = jnp.concatenate([(device - offset) * row_count + row_ids for offset in offsets] + [own_pos])
    distance = own_pos[:, None] - key_pos[None, :]
    visible = ((distance >= 0) & (distance < left_span) & (key_pos[None, :] >= 0))[None]
    key_heads = split_heads(window[:, :ATT])
    value_heads = split_heads(window[:, ATT:])

    scores = (
        jnp.einsum("qhd,khd->hqk", query_heads, key_heads, preferred_element_type=jnp.float32)
        * score_scale
    )
    scores = jnp.where(visible, scores, NEGATIVE)
    row_max = jnp.max(scores, axis=-1)
    weights = jnp.where(visible, jnp.exp(scores - row_max[..., None]), 0.0)
    row_sum = jnp.sum(weights, axis=-1)
    weighted = jnp.einsum(
        "hqk,khd->qhd", weights.astype(jnp.bfloat16), value_heads, preferred_element_type=jnp.float32
    )
    attended = (weighted / jnp.transpose(row_sum)[:, :, None]).astype(jnp.bfloat16)
    log_sums = row_max + jnp.log(row_sum)
    flat = attended.reshape(row_count, ATT)

    hidden = jnp.dot(flat, out_weight, preferred_element_type=jnp.float32).astype(jnp.bfloat16)
    before = from_behind(hidden[-edge_rows:], "blk", 1)
    following = from_behind(
        jnp.concatenate([hidden[:edge_rows], cotangent[0][:edge_rows]], axis=1), "blk", -1
    )
    width = hidden.shape[1]
    extended = jnp.concatenate([before, hidden, following[:, :width]], axis=0).astype(jnp.float32)
    mixed_all = depthwise(extended, conv_kernel, row_count + edge_rows, False)
    sigma_all = jax.nn.sigmoid(mixed_all)
    upstream = jnp.concatenate([cotangent[0], following[:, width:]], axis=0).astype(jnp.float32)
    dmixed_all = upstream * sigma_all * (1.0 + mixed_all * (1.0 - sigma_all))
    out_frames = (mixed_all[:row_count] * sigma_all[:row_count]).astype(jnp.bfloat16)[None]
    dmixed = dmixed_all[:row_count]
    dhidden = depthwise(dmixed_all, conv_kernel, row_count, True).astype(jnp.bfloat16)

    kernel_part = kernel_taps(dmixed, extended[: row_count + edge_rows], edge_rows + 1)
    weight_part = jnp.einsum("ra,rd->ad", flat, dhidden, preferred_element_type=jnp.float32)
    weight_total, kernel_total = sum_weights(weight_part, kernel_part, edge_rows + 1)

    dattended = jnp.einsum(
        "rd,ad->ra", dhidden, out_weight, preferred_element_type=jnp.float32
    ).astype(jnp.bfloat16)
    dout_heads = split_heads(dattended)
    deltas = jnp.einsum("rhe,rhe->hr", dout_heads, attended, preferred_element_type=jnp.float32)

    probs = jnp.where(visible, jnp.exp(scores - log_sums[..., None]), 0.0)
    dvalue_heads = jnp.einsum(
        "hqk,qhd->khd", probs.astype(jnp.bfloat16), dout_heads, preferred_element_type=jnp.float32
    )
    dprobs = jnp.einsum("qhd,khd->hqk", dout_heads, value_heads, preferred_element_type=jnp.float32)
    dscores = (probs * (dprobs - deltas[..., None])).astype(jnp.bfloat16)
    dquery = (
        jnp.einsum("hqk,khd->qhd", dscores, key_heads, preferred_element_type=jnp.float32)
        * score_scale
    )
    dkey_heads = (
        jnp.einsum("hqk,qhd->khd", dscores, query_heads, preferred_element_type=jnp.float32)
        * score_scale
    )
    window_rows = window.shape[0]
    dkv = jnp.concatenate(
        [dkey_heads.reshape(window_rows, ATT), dvalue_heads.reshape(window_rows, ATT)], axis=1
    )
    dkv_total = dkv[context * row_count:]
    for slot, offset in enumerate(offsets):
        part = dkv[slot * row_count:(slot + 1) * row_count].astype(jnp.bfloat16)
        dkv_total = dkv_total + from_behind(part, "blk", -offset).astype(jnp.float32)

    query_grad = dquery.reshape(row_count, ATT).astype(jnp.bfloat16)[None]
    key_grad = dkv_total[:, :ATT].astype(jnp.bfloat16)[None]
    value_grad = dkv_total[:, ATT:].astype(jnp.bfloat16)[None]
    return (out_frames, query_grad, key_grad, value_grad, weight_total, kernel_total)


def solution(mesh):
    return jax.shard_map(
        per_device,
        mesh=mesh,
        in_specs=(
            P("dp", "blk", None),
            P("dp", "blk", None),
            P("dp", "blk", None),
            P(),
            P(),
            P("dp", "blk", None),
        ),
        out_specs=(
            P("dp", "blk", None),
            P("dp", "blk", None),
            P("dp", "blk", None),
            P("dp", "blk", None),
            P(),
            P(),
        ),
        check_vma=False,
    )
```

```python
import functools
import math

import jax
import jax.numpy as jnp
from jax import lax
from jax.experimental import pallas as pl
from jax.experimental.pallas import tpu as pltpu
from jax.sharding import PartitionSpec as P

ATT_HEADS = 8
HEAD_DIM = 64
CTX_MAX = 3
ATT = 512


NEGATIVE = -1e30
MESH_ID = pl.DeviceIdType.MESH


def reduce_bits(dp_size, blk_size):
    if dp_size == 4 and blk_size == 128:
        core0 = [("dp", 1), ("dp", 2), ("blk", 16), ("blk", 2), ("blk", 32),
                 ("blk", 4), ("blk", 64), ("blk", 8), ("blk", 1)]
        core1 = [("dp", 1), ("blk", 16), ("dp", 2), ("blk", 32), ("blk", 2),
                 ("blk", 64), ("blk", 4), ("blk", 1), ("blk", 8)]
        return list(zip(core0, core1))
    bits = []
    for axis, size in (("dp", dp_size), ("blk", blk_size)):
        m = 1
        while m < size:
            bits.append(((axis, m), (axis, m)))
            m *= 2
    return bits


def allreduce_kernel(bits, splits, n_arrays, *refs):
    x_refs = refs[:n_arrays]
    o_refs = refs[n_arrays:2 * n_arrays]
    scratch = refs[2 * n_arrays:]
    n_halve = len(splits)
    halves = [scratch[s * n_arrays:(s + 1) * n_arrays] for s in range(n_halve)]
    base = n_halve * n_arrays
    n_double = len(bits) - n_halve
    doubles = [scratch[base + t * n_arrays:base + (t + 1) * n_arrays] for t in range(n_double)]
    base += n_double * n_arrays
    accs = scratch[base:base + n_arrays]
    send_sem, recv_sem = scratch[base + n_arrays:]
    me = {"dp": lax.axis_index("dp"), "blk": lax.axis_index("blk")}
    core = me["dp"] % 2

    def one_partner(axis, m):
        bit = (me[axis] // m) % 2
        peer = me[axis] + m - 2 * m * bit
        ids = (peer, me["blk"]) if axis == "dp" else (me["dp"], peer)
        return bit, ids

    def partner(specs):
        bit0, ids0 = one_partner(*specs[0])
        bit1, ids1 = one_partner(*specs[1])
        bit = bit0 + (bit1 - bit0) * core
        ids = tuple(a + (b - a) * core for a, b in zip(ids0, ids1))
        return bit, ids

    def window(ref, region):
        r0, rl, c0, cl = region
        return ref.at[pl.ds(pl.multiple_of(r0, 8), rl), pl.ds(pl.multiple_of(c0, 128), cl)]

    def exchange(step, ids, sources, targets, regions):
        copies = []
        for i in range(n_arrays):
            copy = pltpu.make_async_remote_copy(
                src_ref=window(sources[i], regions[i]), dst_ref=targets[i],
                send_sem=send_sem.at[step, i], recv_sem=recv_sem.at[step, i],
                device_id=ids, device_id_type=MESH_ID)
            copy.start()
            copies.append(copy)
        for copy in copies:
            copy.wait()

    barrier = pltpu.get_barrier_semaphore()
    for specs in bits:
        pl.semaphore_signal(barrier, 1, device_id=partner(specs)[1], device_id_type=MESH_ID)
    pl.semaphore_wait(barrier, len(bits))

    regions = [(0, x.shape[0], 0, x.shape[1]) for x in x_refs]
    plan = []
    for step, dim in enumerate(splits):
        bit, ids = partner(bits[step])
        keeps, gives = [], []
        for r0, rl, c0, cl in regions:
            if dim == 0:
                half = rl // 2
                keeps.append((r0 + bit * half, half, c0, cl))
                gives.append((r0 + (1 - bit) * half, half, c0, cl))
            else:
                half = cl // 2
                keeps.append((r0, rl, c0 + bit * half, half))
                gives.append((r0, rl, c0 + (1 - bit) * half, half))
        sources = x_refs if step == 0 else accs
        exchange(step, ids, sources, [h.at[...] for h in halves[step]], gives)
        for i in range(n_arrays):
            window(accs[i], keeps[i])[...] = window(sources[i], keeps[i])[...] + halves[step][i][...]
        plan.append((ids, keeps))
        regions = keeps
    for slot in range(n_double):
        step = n_halve + slot
        bit, ids = partner(bits[step])
        exchange(step, ids, accs, [d.at[...] for d in doubles[slot]], regions)
        for i in range(n_arrays):
            window(accs[i], regions[i])[...] = window(accs[i], regions[i])[...] + doubles[slot][i][...]
    for i in range(n_arrays):
        window(o_refs[i], regions[i])[...] = window(accs[i], regions[i])[...]
    for back, (ids, keeps) in enumerate(reversed(plan)):
        step = len(bits) + back
        exchange(step, ids, o_refs, [window(o, k) for o, k in zip(o_refs, keeps)], keeps)


def allreduce(arrays, dp_size, blk_size, n_halve_max=5):
    bits = reduce_bits(dp_size, blk_size)
    limit = min(n_halve_max, len(bits))
    splits = []
    cols = arrays[0].shape[1]
    rows = [a.shape[0] for a in arrays]
    while len(splits) < limit and cols % 256 == 0:
        splits.append(1)
        cols //= 2
    while len(splits) < limit and all(r % 16 == 0 for r in rows):
        splits.append(0)
        rows = [r // 2 for r in rows]
    scratch = []
    shapes = [a.shape for a in arrays]
    for dim in splits:
        shapes = [(s[0] // 2, s[1]) if dim == 0 else (s[0], s[1] // 2) for s in shapes]
        scratch += [pltpu.VMEM(s, jnp.float32) for s in shapes]
    for _ in bits[len(splits):]:
        scratch += [pltpu.VMEM(s, jnp.float32) for s in shapes]
    scratch += [pltpu.VMEM(a.shape, jnp.float32) for a in arrays]
    steps = len(bits) + len(splits)
    scratch += [pltpu.SemaphoreType.DMA((steps, len(arrays))), pltpu.SemaphoreType.DMA((steps, len(arrays)))]
    return pl.pallas_call(
        functools.partial(allreduce_kernel, bits, splits, len(arrays)),
        out_shape=[jax.ShapeDtypeStruct(a.shape, jnp.float32) for a in arrays],
        in_specs=[pl.BlockSpec(memory_space=pltpu.VMEM)] * len(arrays),
        out_specs=[pl.BlockSpec(memory_space=pltpu.VMEM)] * len(arrays),
        scratch_shapes=scratch,
        compiler_params=pltpu.CompilerParams(collective_id=0, has_side_effects=True),
    )(*arrays)


def halo_body(edge_right_ref, edge_left_ref, before_ref, following_ref, send_sem, recv_sem):
    count = lax.axis_size("blk")
    me = lax.axis_index("blk")
    dp = lax.axis_index("dp")
    has_left = (me + count - 1) // count
    has_right = (2 * count - 2 - me) // count
    left = (dp, (me + count - 1) % count)
    right = (dp, (me + 1) % count)
    barrier = pltpu.get_barrier_semaphore()

    @pl.when(has_left == 1)
    def _():
        pl.semaphore_signal(barrier, 1, device_id=left, device_id_type=MESH_ID)

    @pl.when(has_right == 1)
    def _():
        pl.semaphore_signal(barrier, 1, device_id=right, device_id_type=MESH_ID)

    pl.semaphore_wait(barrier, has_left + has_right)
    to_right = pltpu.make_async_remote_copy(
        src_ref=edge_right_ref, dst_ref=before_ref, send_sem=send_sem.at[0],
        recv_sem=recv_sem.at[0], device_id=right, device_id_type=MESH_ID)
    to_left = pltpu.make_async_remote_copy(
        src_ref=edge_left_ref, dst_ref=following_ref, send_sem=send_sem.at[1],
        recv_sem=recv_sem.at[1], device_id=left, device_id_type=MESH_ID)

    @pl.when(has_right == 1)
    def _():
        to_right.start()

    @pl.when(has_left == 1)
    def _():
        to_left.start()

    @pl.when(has_left == 0)
    def _():
        before_ref[...] = jnp.zeros(before_ref.shape, before_ref.dtype)

    @pl.when(has_right == 0)
    def _():
        following_ref[...] = jnp.zeros(following_ref.shape, following_ref.dtype)

    @pl.when(has_right == 1)
    def _():
        to_right.wait_send()
        to_left.wait_recv()

    @pl.when(has_left == 1)
    def _():
        to_left.wait_send()
        to_right.wait_recv()


def halo_exchange(edge_right, edge_left):
    return pl.pallas_call(
        halo_body,
        out_shape=[jax.ShapeDtypeStruct(edge_right.shape, edge_right.dtype),
                   jax.ShapeDtypeStruct(edge_left.shape, edge_left.dtype)],
        in_specs=[pl.BlockSpec(memory_space=pltpu.VMEM)] * 2,
        out_specs=[pl.BlockSpec(memory_space=pltpu.VMEM)] * 2,
        scratch_shapes=[pltpu.SemaphoreType.DMA((2,)), pltpu.SemaphoreType.DMA((2,))],
        compiler_params=pltpu.CompilerParams(collective_id=1, has_side_effects=True),
    )(edge_right, edge_left)


def from_behind(block, axis, distance):
    devices = range(lax.axis_size(axis))
    route = [(i - distance, i) for i in devices if i - distance in devices]
    return lax.ppermute(block, axis, route)


def split_heads(matrix):
    return matrix.reshape(matrix.shape[0], ATT_HEADS, HEAD_DIM)


def depthwise(extended, conv_kernel, row_count, ahead):
    tap_count = conv_kernel.shape[0]
    total = None
    for tap_index in range(tap_count):
        first_row = tap_index if ahead else tap_count - 1 - tap_index
        term = conv_kernel[tap_index] * extended[first_row:first_row + row_count]
        total = term if total is None else total + term
    return total


def kernel_taps_body(tap_count, dmixed_ref, extended_ref, out_ref):
    rows = dmixed_ref.shape[0]
    first = tap_count - 1
    grads = dmixed_ref[...]
    shifted = []
    for shift in range(8):
        span = (first - shift) // 8 * 8 + rows if shift <= first else 0
        shifted.append(extended_ref[pl.ds(shift, span), :] if span else None)
    for tap in range(tap_count):
        block, shift = divmod(first - tap, 8)
        window = shifted[shift][block * 8:block * 8 + rows]
        out_ref[pl.ds(tap, 1), :] = jnp.sum(grads * window, axis=0, keepdims=True)
    out_ref[pl.ds(tap_count, out_ref.shape[0] - tap_count), :] = jnp.zeros(
        (out_ref.shape[0] - tap_count, out_ref.shape[1]), jnp.float32
    )


def kernel_taps(dmixed, extended, tap_count):
    padded = -(-tap_count // 8) * 8
    return pl.pallas_call(
        functools.partial(kernel_taps_body, tap_count),
        out_shape=jax.ShapeDtypeStruct((padded, dmixed.shape[1]), jnp.float32),
        in_specs=[pl.BlockSpec(memory_space=pltpu.VMEM)] * 2,
        out_specs=pl.BlockSpec(memory_space=pltpu.VMEM),
    )(dmixed, extended)


def sum_weights(weight_part, kernel_part, kernel_rows):
    weight_total, kernel_total = allreduce(
        [weight_part, kernel_part], lax.axis_size("dp"), lax.axis_size("blk")
    )
    return weight_total, kernel_total[:kernel_rows]


def per_device(queries, key_in, value_in, out_weight, conv_kernel, cotangent):
    cycle_count = lax.axis_size("blk")
    device = lax.axis_index("blk")
    row_count = queries.shape[1]
    context = min(CTX_MAX, cycle_count // 4)
    left_span = context * row_count
    score_scale = 1.0 / math.sqrt(HEAD_DIM)
    edge_rows = conv_kernel.shape[0] - 1
    row_ids = jnp.arange(row_count, dtype=jnp.int32)
    query_heads = split_heads(queries[0])
    own_tile = jnp.concatenate([key_in[0], value_in[0]], axis=1)
    own_pos = device * row_count + row_ids

    offsets = list(range(context, 0, -1))
    window = jnp.concatenate(
        [from_behind(own_tile, "blk", offset) for offset in offsets] + [own_tile], axis=0
    )
    key_pos = jnp.concatenate([(device - offset) * row_count + row_ids for offset in offsets] + [own_pos])
    distance = own_pos[:, None] - key_pos[None, :]
    visible = ((distance >= 0) & (distance < left_span) & (key_pos[None, :] >= 0))[None]
    key_heads = split_heads(window[:, :ATT])
    value_heads = split_heads(window[:, ATT:])

    scores = (
        jnp.einsum("qhd,khd->hqk", query_heads, key_heads, preferred_element_type=jnp.float32)
        * score_scale
    )
    scores = jnp.where(visible, scores, NEGATIVE)
    row_max = jnp.max(scores, axis=-1)
    weights = jnp.where(visible, jnp.exp(scores - row_max[..., None]), 0.0)
    row_sum = jnp.sum(weights, axis=-1)
    weighted = jnp.einsum(
        "hqk,khd->qhd", weights.astype(jnp.bfloat16), value_heads, preferred_element_type=jnp.float32
    )
    attended = (weighted / jnp.transpose(row_sum)[:, :, None]).astype(jnp.bfloat16)
    log_sums = row_max + jnp.log(row_sum)
    flat = attended.reshape(row_count, ATT)

    hidden = jnp.dot(flat, out_weight, preferred_element_type=jnp.float32).astype(jnp.bfloat16)
    before, following = halo_exchange(
        hidden[-edge_rows:],
        jnp.concatenate([hidden[:edge_rows], cotangent[0][:edge_rows]], axis=1),
    )
    width = hidden.shape[1]
    extended = jnp.concatenate([before, hidden, following[:, :width]], axis=0).astype(jnp.float32)
    mixed_all = depthwise(extended, conv_kernel, row_count + edge_rows, False)
    sigma_all = jax.nn.sigmoid(mixed_all)
    upstream = jnp.concatenate([cotangent[0], following[:, width:]], axis=0).astype(jnp.float32)
    dmixed_all = upstream * sigma_all * (1.0 + mixed_all * (1.0 - sigma_all))
    out_frames = (mixed_all[:row_count] * sigma_all[:row_count]).astype(jnp.bfloat16)[None]
    dmixed = dmixed_all[:row_count]
    dhidden = depthwise(dmixed_all, conv_kernel, row_count, True).astype(jnp.bfloat16)

    kernel_part = kernel_taps(dmixed, extended[: row_count + edge_rows], edge_rows + 1)
    weight_part = jnp.einsum("ra,rd->ad", flat, dhidden, preferred_element_type=jnp.float32)
    weight_total, kernel_total = sum_weights(weight_part, kernel_part, edge_rows + 1)

    dattended = jnp.einsum(
        "rd,ad->ra", dhidden, out_weight, preferred_element_type=jnp.float32
    ).astype(jnp.bfloat16)
    dout_heads = split_heads(dattended)
    deltas = jnp.einsum("rhe,rhe->hr", dout_heads, attended, preferred_element_type=jnp.float32)

    probs = jnp.where(visible, jnp.exp(scores - log_sums[..., None]), 0.0)
    dvalue_heads = jnp.einsum(
        "hqk,qhd->khd", probs.astype(jnp.bfloat16), dout_heads, preferred_element_type=jnp.float32
    )
    dprobs = jnp.einsum("qhd,khd->hqk", dout_heads, value_heads, preferred_element_type=jnp.float32)
    dscores = (probs * (dprobs - deltas[..., None])).astype(jnp.bfloat16)
    dquery = (
        jnp.einsum("hqk,khd->qhd", dscores, key_heads, preferred_element_type=jnp.float32)
        * score_scale
    )
    dkey_heads = (
        jnp.einsum("hqk,qhd->khd", dscores, query_heads, preferred_element_type=jnp.float32)
        * score_scale
    )
    window_rows = window.shape[0]
    dkv = jnp.concatenate(
        [dkey_heads.reshape(window_rows, ATT), dvalue_heads.reshape(window_rows, ATT)], axis=1
    )
    dkv_total = dkv[context * row_count:]
    for slot, offset in enumerate(offsets):
        part = dkv[slot * row_count:(slot + 1) * row_count].astype(jnp.bfloat16)
        dkv_total = dkv_total + from_behind(part, "blk", -offset).astype(jnp.float32)

    query_grad = dquery.reshape(row_count, ATT).astype(jnp.bfloat16)[None]
    key_grad = dkv_total[:, :ATT].astype(jnp.bfloat16)[None]
    value_grad = dkv_total[:, ATT:].astype(jnp.bfloat16)[None]
    return (out_frames, query_grad, key_grad, value_grad, weight_total, kernel_total)


def solution(mesh):
    return jax.shard_map(
        per_device,
        mesh=mesh,
        in_specs=(
            P("dp", "blk", None),
            P("dp", "blk", None),
            P("dp", "blk", None),
            P(),
            P(),
            P("dp", "blk", None),
        ),
        out_specs=(
            P("dp", "blk", None),
            P("dp", "blk", None),
            P("dp", "blk", None),
            P("dp", "blk", None),
            P(),
            P(),
        ),
        check_vma=False,
    )
```

```python
import functools
import math

import jax
import jax.numpy as jnp
from jax import lax
from jax.experimental import pallas as pl
from jax.experimental.pallas import tpu as pltpu
from jax.sharding import PartitionSpec as P

ATT_HEADS = 8
HEAD_DIM = 64
CTX_MAX = 3
ATT = 512


NEGATIVE = -1e30
MESH_ID = pl.DeviceIdType.MESH


def reduce_bits(dp_size, blk_size):
    if dp_size == 4 and blk_size == 128:
        core0 = [("dp", 1), ("dp", 2), ("blk", 16), ("blk", 2), ("blk", 32),
                 ("blk", 4), ("blk", 64), ("blk", 8), ("blk", 1)]
        core1 = [("dp", 1), ("blk", 16), ("dp", 2), ("blk", 32), ("blk", 2),
                 ("blk", 64), ("blk", 4), ("blk", 1), ("blk", 8)]
        return list(zip(core0, core1))
    bits = []
    for axis, size in (("dp", dp_size), ("blk", blk_size)):
        m = 1
        while m < size:
            bits.append(((axis, m), (axis, m)))
            m *= 2
    return bits


def allreduce_kernel(bits, splits, n_arrays, *refs):
    x_refs = refs[:n_arrays]
    o_refs = refs[n_arrays:2 * n_arrays]
    scratch = refs[2 * n_arrays:]
    n_halve = len(splits)
    halves = [scratch[s * n_arrays:(s + 1) * n_arrays] for s in range(n_halve)]
    base = n_halve * n_arrays
    n_double = len(bits) - n_halve
    doubles = [scratch[base + t * n_arrays:base + (t + 1) * n_arrays] for t in range(n_double // 2)]
    base += n_double // 2 * n_arrays
    accs = scratch[base:base + n_arrays]
    send_sem, recv_sem = scratch[base + n_arrays:]
    me = {"dp": lax.axis_index("dp"), "blk": lax.axis_index("blk")}
    core = me["dp"] % 2

    def one_partner(axis, m):
        bit = (me[axis] // m) % 2
        peer = me[axis] + m - 2 * m * bit
        ids = (peer, me["blk"]) if axis == "dp" else (me["dp"], peer)
        return bit, ids

    def partner(specs):
        bit0, ids0 = one_partner(*specs[0])
        bit1, ids1 = one_partner(*specs[1])
        bit = bit0 + (bit1 - bit0) * core
        ids = tuple(a + (b - a) * core for a, b in zip(ids0, ids1))
        return bit, ids

    def window(ref, region):
        r0, rl, c0, cl = region
        return ref.at[pl.ds(pl.multiple_of(r0, 8), rl), pl.ds(pl.multiple_of(c0, 128), cl)]

    def exchange(step, ids, sources, targets, regions):
        copies = []
        for i in range(n_arrays):
            copy = pltpu.make_async_remote_copy(
                src_ref=window(sources[i], regions[i]), dst_ref=targets[i],
                send_sem=send_sem.at[step, i, 0], recv_sem=recv_sem.at[step, i, 0],
                device_id=ids, device_id_type=MESH_ID)
            copy.start()
            copies.append(copy)
        for copy in copies:
            copy.wait()

    def diagonal_of(step):
        ids_a = partner(bits[step])[1]
        ids_b = partner(bits[step + 1])[1]
        return tuple(a + b - m for a, b, m in zip(ids_a, ids_b, (me["dp"], me["blk"])))

    n_groups = (len(bits) - n_halve) // 2
    barrier = pltpu.get_barrier_semaphore()
    for specs in bits:
        pl.semaphore_signal(barrier, 1, device_id=partner(specs)[1], device_id_type=MESH_ID)
    for pair in range(n_groups):
        pl.semaphore_signal(barrier, 1, device_id=diagonal_of(n_halve + 2 * pair), device_id_type=MESH_ID)
    pl.semaphore_wait(barrier, len(bits) + n_groups)

    regions = [(0, x.shape[0], 0, x.shape[1]) for x in x_refs]
    plan = []
    for step, dim in enumerate(splits):
        bit, ids = partner(bits[step])
        keeps, gives = [], []
        for r0, rl, c0, cl in regions:
            if dim == 0:
                half = rl // 2
                keeps.append((r0 + bit * half, half, c0, cl))
                gives.append((r0 + (1 - bit) * half, half, c0, cl))
            else:
                half = cl // 2
                keeps.append((r0, rl, c0 + bit * half, half))
                gives.append((r0, rl, c0 + (1 - bit) * half, half))
        sources = x_refs if step == 0 else accs
        exchange(step, ids, sources, [h.at[...] for h in halves[step]], gives)
        for i in range(n_arrays):
            window(accs[i], keeps[i])[...] = window(sources[i], keeps[i])[...] + halves[step][i][...]
        plan.append((ids, keeps))
        regions = keeps
    for pair in range(n_double // 2):
        step = n_halve + 2 * pair
        bit_a, ids_a = partner(bits[step])
        bit_b, ids_b = partner(bits[step + 1])
        place = bit_a + 2 * bit_b
        diagonal = diagonal_of(step)
        slots = doubles[pair]
        for i in range(n_arrays):
            own = pltpu.make_async_copy(
                window(accs[i], regions[i]), slots[i].at[place], recv_sem.at[step, i, place])
            own.start()
            for k, ids in enumerate((ids_a, ids_b, diagonal)):
                copy = pltpu.make_async_remote_copy(
                    src_ref=window(accs[i], regions[i]), dst_ref=slots[i].at[place],
                    send_sem=send_sem.at[step, i, k], recv_sem=recv_sem.at[step, i, place],
                    device_id=ids, device_id_type=MESH_ID)
                copy.start()
        for i in range(n_arrays):
            for k in range(3):
                pltpu.make_async_remote_copy(
                    src_ref=window(accs[i], regions[i]), dst_ref=slots[i].at[0],
                    send_sem=send_sem.at[step, i, k], recv_sem=recv_sem.at[step, i, 0],
                    device_id=ids_a, device_id_type=MESH_ID).wait_send()
            for g in range(4):
                pltpu.make_async_copy(
                    window(accs[i], regions[i]), slots[i].at[g], recv_sem.at[step, i, g]).wait()
        for i in range(n_arrays):
            total = slots[i][0] + slots[i][1]
            total = total + slots[i][2]
            window(accs[i], regions[i])[...] = total + slots[i][3]
    for i in range(n_arrays):
        window(o_refs[i], regions[i])[...] = window(accs[i], regions[i])[...]
    for back, (ids, keeps) in enumerate(reversed(plan)):
        step = len(bits) + back
        exchange(step, ids, o_refs, [window(o, k) for o, k in zip(o_refs, keeps)], keeps)


def allreduce(arrays, dp_size, blk_size, n_halve_max=5):
    bits = reduce_bits(dp_size, blk_size)
    limit = min(n_halve_max, len(bits))
    splits = []
    cols = arrays[0].shape[1]
    rows = [a.shape[0] for a in arrays]
    while len(splits) < limit and cols % 256 == 0:
        splits.append(1)
        cols //= 2
    while len(splits) < limit and all(r % 16 == 0 for r in rows):
        splits.append(0)
        rows = [r // 2 for r in rows]
    scratch = []
    shapes = [a.shape for a in arrays]
    for dim in splits:
        shapes = [(s[0] // 2, s[1]) if dim == 0 else (s[0], s[1] // 2) for s in shapes]
        scratch += [pltpu.VMEM(s, jnp.float32) for s in shapes]
    for _ in range((len(bits) - len(splits)) // 2):
        scratch += [pltpu.VMEM((4,) + s, jnp.float32) for s in shapes]
    scratch += [pltpu.VMEM(a.shape, jnp.float32) for a in arrays]
    steps = len(bits) + len(splits)
    sems = (steps, len(arrays), 4)
    scratch += [pltpu.SemaphoreType.DMA(sems), pltpu.SemaphoreType.DMA(sems)]
    return pl.pallas_call(
        functools.partial(allreduce_kernel, bits, splits, len(arrays)),
        out_shape=[jax.ShapeDtypeStruct(a.shape, jnp.float32) for a in arrays],
        in_specs=[pl.BlockSpec(memory_space=pltpu.VMEM)] * len(arrays),
        out_specs=[pl.BlockSpec(memory_space=pltpu.VMEM)] * len(arrays),
        scratch_shapes=scratch,
        compiler_params=pltpu.CompilerParams(collective_id=0, has_side_effects=True),
    )(*arrays)


def from_behind(block, axis, distance):
    devices = range(lax.axis_size(axis))
    route = [(i - distance, i) for i in devices if i - distance in devices]
    return lax.ppermute(block, axis, route)


def split_heads(matrix):
    return matrix.reshape(matrix.shape[0], ATT_HEADS, HEAD_DIM)


def depthwise(extended, conv_kernel, row_count, ahead):
    tap_count = conv_kernel.shape[0]
    total = None
    for tap_index in range(tap_count):
        first_row = tap_index if ahead else tap_count - 1 - tap_index
        term = conv_kernel[tap_index] * extended[first_row:first_row + row_count]
        total = term if total is None else total + term
    return total


def kernel_taps_body(tap_count, dmixed_ref, extended_ref, out_ref):
    rows = dmixed_ref.shape[0]
    first = tap_count - 1
    grads = dmixed_ref[...]
    shifted = []
    for shift in range(8):
        span = (first - shift) // 8 * 8 + rows if shift <= first else 0
        shifted.append(extended_ref[pl.ds(shift, span), :] if span else None)
    for tap in range(tap_count):
        block, shift = divmod(first - tap, 8)
        window = shifted[shift][block * 8:block * 8 + rows]
        out_ref[pl.ds(tap, 1), :] = jnp.sum(grads * window, axis=0, keepdims=True)
    out_ref[pl.ds(tap_count, out_ref.shape[0] - tap_count), :] = jnp.zeros(
        (out_ref.shape[0] - tap_count, out_ref.shape[1]), jnp.float32
    )


def kernel_taps(dmixed, extended, tap_count):
    padded = -(-tap_count // 8) * 8
    return pl.pallas_call(
        functools.partial(kernel_taps_body, tap_count),
        out_shape=jax.ShapeDtypeStruct((padded, dmixed.shape[1]), jnp.float32),
        in_specs=[pl.BlockSpec(memory_space=pltpu.VMEM)] * 2,
        out_specs=pl.BlockSpec(memory_space=pltpu.VMEM),
    )(dmixed, extended)


def sum_weights(weight_part, kernel_part, kernel_rows):
    weight_total, kernel_total = allreduce(
        [weight_part, kernel_part], lax.axis_size("dp"), lax.axis_size("blk")
    )
    return weight_total, kernel_total[:kernel_rows]


def per_device(queries, key_in, value_in, out_weight, conv_kernel, cotangent):
    cycle_count = lax.axis_size("blk")
    device = lax.axis_index("blk")
    row_count = queries.shape[1]
    context = min(CTX_MAX, cycle_count // 4)
    left_span = context * row_count
    score_scale = 1.0 / math.sqrt(HEAD_DIM)
    edge_rows = conv_kernel.shape[0] - 1
    row_ids = jnp.arange(row_count, dtype=jnp.int32)
    query_heads = split_heads(queries[0])
    own_tile = jnp.concatenate([key_in[0], value_in[0]], axis=1)
    own_pos = device * row_count + row_ids

    offsets = list(range(context, 0, -1))
    window = jnp.concatenate(
        [from_behind(own_tile, "blk", offset) for offset in offsets] + [own_tile], axis=0
    )
    key_pos = jnp.concatenate([(device - offset) * row_count + row_ids for offset in offsets] + [own_pos])
    distance = own_pos[:, None] - key_pos[None, :]
    visible = ((distance >= 0) & (distance < left_span) & (key_pos[None, :] >= 0))[None]
    key_heads = split_heads(window[:, :ATT])
    value_heads = split_heads(window[:, ATT:])

    scores = (
        jnp.einsum("qhd,khd->hqk", query_heads, key_heads, preferred_element_type=jnp.float32)
        * score_scale
    )
    scores = jnp.where(visible, scores, NEGATIVE)
    row_max = jnp.max(scores, axis=-1)
    weights = jnp.where(visible, jnp.exp(scores - row_max[..., None]), 0.0)
    row_sum = jnp.sum(weights, axis=-1)
    weighted = jnp.einsum(
        "hqk,khd->qhd", weights.astype(jnp.bfloat16), value_heads, preferred_element_type=jnp.float32
    )
    attended = (weighted / jnp.transpose(row_sum)[:, :, None]).astype(jnp.bfloat16)
    log_sums = row_max + jnp.log(row_sum)
    flat = attended.reshape(row_count, ATT)

    hidden = jnp.dot(flat, out_weight, preferred_element_type=jnp.float32).astype(jnp.bfloat16)
    before = from_behind(hidden[-edge_rows:], "blk", 1)
    following = from_behind(
        jnp.concatenate([hidden[:edge_rows], cotangent[0][:edge_rows]], axis=1), "blk", -1
    )
    width = hidden.shape[1]
    extended = jnp.concatenate([before, hidden, following[:, :width]], axis=0).astype(jnp.float32)
    mixed_all = depthwise(extended, conv_kernel, row_count + edge_rows, False)
    sigma_all = jax.nn.sigmoid(mixed_all)
    upstream = jnp.concatenate([cotangent[0], following[:, width:]], axis=0).astype(jnp.float32)
    dmixed_all = upstream * sigma_all * (1.0 + mixed_all * (1.0 - sigma_all))
    out_frames = (mixed_all[:row_count] * sigma_all[:row_count]).astype(jnp.bfloat16)[None]
    dmixed = dmixed_all[:row_count]
    dhidden = depthwise(dmixed_all, conv_kernel, row_count, True).astype(jnp.bfloat16)

    kernel_part = kernel_taps(dmixed, extended[: row_count + edge_rows], edge_rows + 1)
    weight_part = jnp.einsum("ra,rd->ad", flat, dhidden, preferred_element_type=jnp.float32)
    weight_total, kernel_total = sum_weights(weight_part, kernel_part, edge_rows + 1)

    dattended = jnp.einsum(
        "rd,ad->ra", dhidden, out_weight, preferred_element_type=jnp.float32
    ).astype(jnp.bfloat16)
    dout_heads = split_heads(dattended)
    deltas = jnp.einsum("rhe,rhe->hr", dout_heads, attended, preferred_element_type=jnp.float32)

    probs = jnp.where(visible, jnp.exp(scores - log_sums[..., None]), 0.0)
    dvalue_heads = jnp.einsum(
        "hqk,qhd->khd", probs.astype(jnp.bfloat16), dout_heads, preferred_element_type=jnp.float32
    )
    dprobs = jnp.einsum("qhd,khd->hqk", dout_heads, value_heads, preferred_element_type=jnp.float32)
    dscores = (probs * (dprobs - deltas[..., None])).astype(jnp.bfloat16)
    dquery = (
        jnp.einsum("hqk,khd->qhd", dscores, key_heads, preferred_element_type=jnp.float32)
        * score_scale
    )
    dkey_heads = (
        jnp.einsum("hqk,qhd->khd", dscores, query_heads, preferred_element_type=jnp.float32)
        * score_scale
    )
    window_rows = window.shape[0]
    dkv = jnp.concatenate(
        [dkey_heads.reshape(window_rows, ATT), dvalue_heads.reshape(window_rows, ATT)], axis=1
    )
    dkv_total = dkv[context * row_count:]
    for slot, offset in enumerate(offsets):
        part = dkv[slot * row_count:(slot + 1) * row_count].astype(jnp.bfloat16)
        dkv_total = dkv_total + from_behind(part, "blk", -offset).astype(jnp.float32)

    query_grad = dquery.reshape(row_count, ATT).astype(jnp.bfloat16)[None]
    key_grad = dkv_total[:, :ATT].astype(jnp.bfloat16)[None]
    value_grad = dkv_total[:, ATT:].astype(jnp.bfloat16)[None]
    return (out_frames, query_grad, key_grad, value_grad, weight_total, kernel_total)


def solution(mesh):
    return jax.shard_map(
        per_device,
        mesh=mesh,
        in_specs=(
            P("dp", "blk", None),
            P("dp", "blk", None),
            P("dp", "blk", None),
            P(),
            P(),
            P("dp", "blk", None),
        ),
        out_specs=(
            P("dp", "blk", None),
            P("dp", "blk", None),
            P("dp", "blk", None),
            P("dp", "blk", None),
            P(),
            P(),
        ),
        check_vma=False,
    )
```

```python
import functools
import math

import jax
import jax.numpy as jnp
from jax import lax
from jax.experimental import pallas as pl
from jax.experimental.pallas import tpu as pltpu
from jax.sharding import PartitionSpec as P

ATT_HEADS = 8
HEAD_DIM = 64
CTX_MAX = 3
ATT = 512


NEGATIVE = -1e30
MESH_ID = pl.DeviceIdType.MESH


def reduce_bits(dp_size, blk_size):
    if dp_size == 4 and blk_size == 128:
        core0 = [("dp", 1), ("dp", 2), ("blk", 16), ("blk", 2), ("blk", 32),
                 ("blk", 4), ("blk", 64), ("blk", 8), ("blk", 1)]
        core1 = [("dp", 1), ("blk", 16), ("dp", 2), ("blk", 32), ("blk", 2),
                 ("blk", 64), ("blk", 4), ("blk", 1), ("blk", 8)]
        return list(zip(core0, core1))
    bits = []
    for axis, size in (("dp", dp_size), ("blk", blk_size)):
        m = 1
        while m < size:
            bits.append(((axis, m), (axis, m)))
            m *= 2
    return bits


def allreduce_kernel(bits, splits, n_arrays, *refs):
    x_refs = refs[:n_arrays]
    o_refs = refs[n_arrays:2 * n_arrays]
    scratch = refs[2 * n_arrays:]
    n_halve = len(splits)
    halves = [scratch[s * n_arrays:(s + 1) * n_arrays] for s in range(n_halve)]
    base = n_halve * n_arrays
    n_double = len(bits) - n_halve
    doubles = [scratch[base + t * n_arrays:base + (t + 1) * n_arrays] for t in range(n_double)]
    base += n_double * n_arrays
    accs = scratch[base:base + n_arrays]
    send_sem, recv_sem = scratch[base + n_arrays:]
    me = {"dp": lax.axis_index("dp"), "blk": lax.axis_index("blk")}
    core = me["dp"] % 2

    def one_partner(axis, m):
        bit = (me[axis] // m) % 2
        peer = me[axis] + m - 2 * m * bit
        ids = (peer, me["blk"]) if axis == "dp" else (me["dp"], peer)
        return bit, ids

    def partner(specs):
        bit0, ids0 = one_partner(*specs[0])
        bit1, ids1 = one_partner(*specs[1])
        bit = bit0 + (bit1 - bit0) * core
        ids = tuple(a + (b - a) * core for a, b in zip(ids0, ids1))
        return bit, ids

    def window(ref, region):
        r0, rl, c0, cl = region
        return ref.at[pl.ds(pl.multiple_of(r0, 8), rl), pl.ds(pl.multiple_of(c0, 128), cl)]

    def exchange(step, ids, sources, targets, regions):
        copies = []
        for i in range(n_arrays):
            copy = pltpu.make_async_remote_copy(
                src_ref=window(sources[i], regions[i]), dst_ref=targets[i],
                send_sem=send_sem.at[step, i], recv_sem=recv_sem.at[step, i],
                device_id=ids, device_id_type=MESH_ID)
            copy.start()
            copies.append(copy)
        for copy in copies:
            copy.wait()

    barrier = pltpu.get_barrier_semaphore()
    for specs in bits:
        pl.semaphore_signal(barrier, 1, device_id=partner(specs)[1], device_id_type=MESH_ID)
    pl.semaphore_wait(barrier, len(bits))

    regions = [(0, x.shape[0], 0, x.shape[1]) for x in x_refs]
    plan = []
    for step, dim in enumerate(splits):
        bit, ids = partner(bits[step])
        keeps, gives = [], []
        for r0, rl, c0, cl in regions:
            if dim == 0:
                half = rl // 2
                keeps.append((r0 + bit * half, half, c0, cl))
                gives.append((r0 + (1 - bit) * half, half, c0, cl))
            else:
                half = cl // 2
                keeps.append((r0, rl, c0 + bit * half, half))
                gives.append((r0, rl, c0 + (1 - bit) * half, half))
        sources = x_refs if step == 0 else accs
        exchange(step, ids, sources, [h.at[...] for h in halves[step]], gives)
        for i in range(n_arrays):
            window(accs[i], keeps[i])[...] = window(sources[i], keeps[i])[...] + halves[step][i][...]
        plan.append((ids, keeps))
        regions = keeps
    for slot in range(n_double):
        step = n_halve + slot
        bit, ids = partner(bits[step])
        exchange(step, ids, accs, [d.at[...] for d in doubles[slot]], regions)
        for i in range(n_arrays):
            window(accs[i], regions[i])[...] = window(accs[i], regions[i])[...] + doubles[slot][i][...]
    for i in range(n_arrays):
        window(o_refs[i], regions[i])[...] = window(accs[i], regions[i])[...]
    for back, (ids, keeps) in enumerate(reversed(plan)):
        step = len(bits) + back
        exchange(step, ids, o_refs, [window(o, k) for o, k in zip(o_refs, keeps)], keeps)


def allreduce(arrays, dp_size, blk_size, n_halve_max=5):
    bits = reduce_bits(dp_size, blk_size)
    limit = min(n_halve_max, len(bits))
    splits = []
    cols = arrays[0].shape[1]
    rows = [a.shape[0] for a in arrays]
    while len(splits) < limit and cols % 256 == 0:
        splits.append(1)
        cols //= 2
    while len(splits) < limit and all(r % 16 == 0 for r in rows):
        splits.append(0)
        rows = [r // 2 for r in rows]
    scratch = []
    shapes = [a.shape for a in arrays]
    for dim in splits:
        shapes = [(s[0] // 2, s[1]) if dim == 0 else (s[0], s[1] // 2) for s in shapes]
        scratch += [pltpu.VMEM(s, jnp.float32) for s in shapes]
    for _ in bits[len(splits):]:
        scratch += [pltpu.VMEM(s, jnp.float32) for s in shapes]
    scratch += [pltpu.VMEM(a.shape, jnp.float32) for a in arrays]
    steps = len(bits) + len(splits)
    scratch += [pltpu.SemaphoreType.DMA((steps, len(arrays))), pltpu.SemaphoreType.DMA((steps, len(arrays)))]
    return pl.pallas_call(
        functools.partial(allreduce_kernel, bits, splits, len(arrays)),
        out_shape=[jax.ShapeDtypeStruct(a.shape, jnp.float32) for a in arrays],
        in_specs=[pl.BlockSpec(memory_space=pltpu.VMEM)] * len(arrays),
        out_specs=[pl.BlockSpec(memory_space=pltpu.VMEM)] * len(arrays),
        scratch_shapes=scratch,
        compiler_params=pltpu.CompilerParams(collective_id=0, has_side_effects=True),
    )(*arrays)


def from_behind(block, axis, distance):
    devices = range(lax.axis_size(axis))
    route = [(i - distance, i) for i in devices if i - distance in devices]
    return lax.ppermute(block, axis, route)


def split_heads(matrix):
    return matrix.reshape(matrix.shape[0], ATT_HEADS, HEAD_DIM)


def depthwise(extended, conv_kernel, row_count, ahead):
    tap_count = conv_kernel.shape[0]
    total = None
    for tap_index in range(tap_count):
        first_row = tap_index if ahead else tap_count - 1 - tap_index
        term = conv_kernel[tap_index] * extended[first_row:first_row + row_count]
        total = term if total is None else total + term
    return total


def kernel_taps_body(tap_count, dmixed_ref, extended_ref, out_ref):
    rows = dmixed_ref.shape[0]
    first = tap_count - 1
    grads = dmixed_ref[...]
    shifted = []
    for shift in range(8):
        span = (first - shift) // 8 * 8 + rows if shift <= first else 0
        shifted.append(extended_ref[pl.ds(shift, span), :] if span else None)
    for tap in range(tap_count):
        block, shift = divmod(first - tap, 8)
        window = shifted[shift][block * 8:block * 8 + rows]
        out_ref[pl.ds(tap, 1), :] = jnp.sum(grads * window, axis=0, keepdims=True)
    out_ref[pl.ds(tap_count, out_ref.shape[0] - tap_count), :] = jnp.zeros(
        (out_ref.shape[0] - tap_count, out_ref.shape[1]), jnp.float32
    )


def kernel_taps(dmixed, extended, tap_count):
    padded = -(-tap_count // 8) * 8
    return pl.pallas_call(
        functools.partial(kernel_taps_body, tap_count),
        out_shape=jax.ShapeDtypeStruct((padded, dmixed.shape[1]), jnp.float32),
        in_specs=[pl.BlockSpec(memory_space=pltpu.VMEM)] * 2,
        out_specs=pl.BlockSpec(memory_space=pltpu.VMEM),
    )(dmixed, extended)


def sum_weights(weight_part, kernel_part, kernel_rows):
    weight_total, kernel_total = allreduce(
        [weight_part, kernel_part], lax.axis_size("dp"), lax.axis_size("blk")
    )
    return weight_total, kernel_total[:kernel_rows]


def per_device(queries, key_in, value_in, out_weight, conv_kernel, cotangent):
    cycle_count = lax.axis_size("blk")
    device = lax.axis_index("blk")
    row_count = queries.shape[1]
    context = min(CTX_MAX, cycle_count // 4)
    left_span = context * row_count
    score_scale = 1.0 / math.sqrt(HEAD_DIM)
    edge_rows = conv_kernel.shape[0] - 1
    row_ids = jnp.arange(row_count, dtype=jnp.int32)
    query_heads = split_heads(queries[0])
    own_tile = jnp.concatenate([key_in[0], value_in[0]], axis=1)
    own_pos = device * row_count + row_ids

    offsets = list(range(context, 0, -1))
    window = jnp.concatenate(
        [from_behind(own_tile, "blk", offset) for offset in offsets] + [own_tile], axis=0
    )
    key_pos = jnp.concatenate([(device - offset) * row_count + row_ids for offset in offsets] + [own_pos])
    distance = own_pos[:, None] - key_pos[None, :]
    visible = ((distance >= 0) & (distance < left_span) & (key_pos[None, :] >= 0))[None]
    key_heads = split_heads(window[:, :ATT])
    value_heads = split_heads(window[:, ATT:])

    scores = (
        jnp.einsum("qhd,khd->hqk", query_heads, key_heads, preferred_element_type=jnp.float32)
        * score_scale
    )
    scores = jnp.where(visible, scores, NEGATIVE)
    row_max = jnp.max(scores, axis=-1)
    weights = jnp.where(visible, jnp.exp(scores - row_max[..., None]), 0.0)
    row_sum = jnp.sum(weights, axis=-1)
    weighted = jnp.einsum(
        "hqk,khd->qhd", weights.astype(jnp.bfloat16), value_heads, preferred_element_type=jnp.float32
    )
    attended = (weighted / jnp.transpose(row_sum)[:, :, None]).astype(jnp.bfloat16)
    log_sums = row_max + jnp.log(row_sum)
    flat = attended.reshape(row_count, ATT)

    hidden = jnp.dot(flat, out_weight, preferred_element_type=jnp.float32).astype(jnp.bfloat16)
    before = from_behind(hidden[-edge_rows:], "blk", 1)
    following = from_behind(
        jnp.concatenate([hidden[:edge_rows], cotangent[0][:edge_rows]], axis=1), "blk", -1
    )
    width = hidden.shape[1]
    extended = jnp.concatenate([before, hidden, following[:, :width]], axis=0).astype(jnp.float32)
    mixed_all = depthwise(extended, conv_kernel, row_count + edge_rows, False)
    sigma_all = jax.nn.sigmoid(mixed_all)
    upstream = jnp.concatenate([cotangent[0], following[:, width:]], axis=0).astype(jnp.float32)
    dmixed_all = upstream * sigma_all * (1.0 + mixed_all * (1.0 - sigma_all))
    out_frames = (mixed_all[:row_count] * sigma_all[:row_count]).astype(jnp.bfloat16)[None]
    dmixed = dmixed_all[:row_count]
    dhidden = depthwise(dmixed_all, conv_kernel, row_count, True).astype(jnp.bfloat16)

    kernel_part = kernel_taps(dmixed, extended[: row_count + edge_rows], edge_rows + 1)
    weight_part = jnp.einsum("ra,rd->ad", flat, dhidden, preferred_element_type=jnp.float32)
    weight_total, kernel_total = sum_weights(weight_part, kernel_part, edge_rows + 1)

    dattended = jnp.einsum(
        "rd,ad->ra", dhidden, out_weight, preferred_element_type=jnp.float32
    ).astype(jnp.bfloat16)
    dout_heads = split_heads(dattended)
    deltas = jnp.einsum("rhe,rhe->hr", dout_heads, attended, preferred_element_type=jnp.float32)

    probs = jnp.where(visible, jnp.exp(scores - log_sums[..., None]), 0.0)
    dvalue_heads = jnp.einsum(
        "hqk,qhd->khd", probs.astype(jnp.bfloat16), dout_heads, preferred_element_type=jnp.float32
    )
    dprobs = jnp.einsum("qhd,khd->hqk", dout_heads, value_heads, preferred_element_type=jnp.float32)
    dscores = (probs * (dprobs - deltas[..., None])).astype(jnp.bfloat16)
    dquery = (
        jnp.einsum("hqk,khd->qhd", dscores, key_heads, preferred_element_type=jnp.float32)
        * score_scale
    )
    dkey_heads = (
        jnp.einsum("hqk,qhd->khd", dscores, query_heads, preferred_element_type=jnp.float32)
        * score_scale
    )
    window_rows = window.shape[0]
    dkv = jnp.concatenate(
        [
            dkey_heads.astype(jnp.bfloat16).reshape(window_rows, ATT),
            dvalue_heads.astype(jnp.bfloat16).reshape(window_rows, ATT),
        ],
        axis=1,
    )
    dkv_total = dkv[context * row_count:].astype(jnp.float32)
    for slot, offset in enumerate(offsets):
        part = dkv[slot * row_count:(slot + 1) * row_count]
        dkv_total = dkv_total + from_behind(part, "blk", -offset).astype(jnp.float32)

    query_grad = dquery.reshape(row_count, ATT).astype(jnp.bfloat16)[None]
    key_grad = dkv_total[:, :ATT].astype(jnp.bfloat16)[None]
    value_grad = dkv_total[:, ATT:].astype(jnp.bfloat16)[None]
    return (out_frames, query_grad, key_grad, value_grad, weight_total, kernel_total)


def solution(mesh):
    return jax.shard_map(
        per_device,
        mesh=mesh,
        in_specs=(
            P("dp", "blk", None),
            P("dp", "blk", None),
            P("dp", "blk", None),
            P(),
            P(),
            P("dp", "blk", None),
        ),
        out_specs=(
            P("dp", "blk", None),
            P("dp", "blk", None),
            P("dp", "blk", None),
            P("dp", "blk", None),
            P(),
            P(),
        ),
        check_vma=False,
    )
```

```python
import functools
import math

import jax
import jax.numpy as jnp
from jax import lax
from jax.experimental import pallas as pl
from jax.experimental.pallas import tpu as pltpu
from jax.sharding import PartitionSpec as P

ATT_HEADS = 8
HEAD_DIM = 64
CTX_MAX = 3
ATT = 512


NEGATIVE = -1e30
MESH_ID = pl.DeviceIdType.MESH


def reduce_bits(dp_size, blk_size):
    if dp_size == 4 and blk_size == 128:
        core0 = [("dp", 1), ("dp", 2), ("blk", 16), ("blk", 2), ("blk", 32),
                 ("blk", 4), ("blk", 64), ("blk", 8), ("blk", 1)]
        core1 = [("dp", 1), ("blk", 16), ("dp", 2), ("blk", 32), ("blk", 2),
                 ("blk", 64), ("blk", 4), ("blk", 1), ("blk", 8)]
        return list(zip(core0, core1))
    bits = []
    for axis, size in (("dp", dp_size), ("blk", blk_size)):
        m = 1
        while m < size:
            bits.append(((axis, m), (axis, m)))
            m *= 2
    return bits


def allreduce_kernel(bits, splits, n_arrays, *refs):
    x_refs = refs[:n_arrays]
    o_refs = refs[n_arrays:2 * n_arrays]
    scratch = refs[2 * n_arrays:]
    n_halve = len(splits)
    halves = [scratch[s * n_arrays:(s + 1) * n_arrays] for s in range(n_halve)]
    base = n_halve * n_arrays
    n_double = len(bits) - n_halve
    doubles = [scratch[base + t * n_arrays:base + (t + 1) * n_arrays] for t in range(n_double)]
    base += n_double * n_arrays
    accs = scratch[base:base + n_arrays]
    send_sem, recv_sem = scratch[base + n_arrays:]
    me = {"dp": lax.axis_index("dp"), "blk": lax.axis_index("blk")}
    core = me["dp"] % 2

    def one_partner(axis, m):
        bit = (me[axis] // m) % 2
        peer = me[axis] + m - 2 * m * bit
        ids = (peer, me["blk"]) if axis == "dp" else (me["dp"], peer)
        return bit, ids

    def partner(specs):
        bit0, ids0 = one_partner(*specs[0])
        bit1, ids1 = one_partner(*specs[1])
        bit = bit0 + (bit1 - bit0) * core
        ids = tuple(a + (b - a) * core for a, b in zip(ids0, ids1))
        return bit, ids

    def window(ref, region):
        r0, rl, c0, cl = region
        return ref.at[pl.ds(pl.multiple_of(r0, 8), rl), pl.ds(pl.multiple_of(c0, 128), cl)]

    def exchange(step, ids, sources, targets, regions):
        copies = []
        for i in range(n_arrays):
            copy = pltpu.make_async_remote_copy(
                src_ref=window(sources[i], regions[i]), dst_ref=targets[i],
                send_sem=send_sem.at[step, i], recv_sem=recv_sem.at[step, i],
                device_id=ids, device_id_type=MESH_ID)
            copy.start()
            copies.append(copy)
        for copy in copies:
            copy.wait()

    barrier = pltpu.get_barrier_semaphore()
    for specs in bits:
        pl.semaphore_signal(barrier, 1, device_id=partner(specs)[1], device_id_type=MESH_ID)
    pl.semaphore_wait(barrier, len(bits))

    regions = [(0, x.shape[0], 0, x.shape[1]) for x in x_refs]
    plan = []
    for step, dim in enumerate(splits):
        bit, ids = partner(bits[step])
        keeps, gives = [], []
        for r0, rl, c0, cl in regions:
            if dim == 0:
                half = rl // 2
                keeps.append((r0 + bit * half, half, c0, cl))
                gives.append((r0 + (1 - bit) * half, half, c0, cl))
            else:
                half = cl // 2
                keeps.append((r0, rl, c0 + bit * half, half))
                gives.append((r0, rl, c0 + (1 - bit) * half, half))
        sources = x_refs if step == 0 else accs
        exchange(step, ids, sources, [h.at[...] for h in halves[step]], gives)
        for i in range(n_arrays):
            window(accs[i], keeps[i])[...] = window(sources[i], keeps[i])[...] + halves[step][i][...]
        plan.append((ids, keeps))
        regions = keeps
    for slot in range(n_double):
        step = n_halve + slot
        bit, ids = partner(bits[step])
        exchange(step, ids, accs, [d.at[...] for d in doubles[slot]], regions)
        for i in range(n_arrays):
            window(accs[i], regions[i])[...] = window(accs[i], regions[i])[...] + doubles[slot][i][...]
    for i in range(n_arrays):
        window(o_refs[i], regions[i])[...] = window(accs[i], regions[i])[...]
    for back, (ids, keeps) in enumerate(reversed(plan)):
        step = len(bits) + back
        exchange(step, ids, o_refs, [window(o, k) for o, k in zip(o_refs, keeps)], keeps)


def allreduce(arrays, dp_size, blk_size, n_halve_max=5):
    bits = reduce_bits(dp_size, blk_size)
    limit = min(n_halve_max, len(bits))
    splits = []
    cols = arrays[0].shape[1]
    rows = [a.shape[0] for a in arrays]
    while len(splits) < limit and cols % 256 == 0:
        splits.append(1)
        cols //= 2
    while len(splits) < limit and all(r % 16 == 0 for r in rows):
        splits.append(0)
        rows = [r // 2 for r in rows]
    scratch = []
    shapes = [a.shape for a in arrays]
    for dim in splits:
        shapes = [(s[0] // 2, s[1]) if dim == 0 else (s[0], s[1] // 2) for s in shapes]
        scratch += [pltpu.VMEM(s, jnp.float32) for s in shapes]
    for _ in bits[len(splits):]:
        scratch += [pltpu.VMEM(s, jnp.float32) for s in shapes]
    scratch += [pltpu.VMEM(a.shape, jnp.float32) for a in arrays]
    steps = len(bits) + len(splits)
    scratch += [pltpu.SemaphoreType.DMA((steps, len(arrays))), pltpu.SemaphoreType.DMA((steps, len(arrays)))]
    return pl.pallas_call(
        functools.partial(allreduce_kernel, bits, splits, len(arrays)),
        out_shape=[jax.ShapeDtypeStruct(a.shape, jnp.float32) for a in arrays],
        in_specs=[pl.BlockSpec(memory_space=pltpu.VMEM)] * len(arrays),
        out_specs=[pl.BlockSpec(memory_space=pltpu.VMEM)] * len(arrays),
        scratch_shapes=scratch,
        compiler_params=pltpu.CompilerParams(collective_id=0, has_side_effects=True),
    )(*arrays)


def from_behind(block, axis, distance):
    devices = range(lax.axis_size(axis))
    route = [(i - distance, i) for i in devices if i - distance in devices]
    return lax.ppermute(block, axis, route)


def split_heads(matrix):
    return matrix.reshape(matrix.shape[0], ATT_HEADS, HEAD_DIM)


def depthwise(extended, conv_kernel, row_count, ahead):
    tap_count = conv_kernel.shape[0]
    total = None
    for tap_index in range(tap_count):
        first_row = tap_index if ahead else tap_count - 1 - tap_index
        term = conv_kernel[tap_index] * extended[first_row:first_row + row_count]
        total = term if total is None else total + term
    return total


def kernel_taps_body(tap_count, dmixed_ref, extended_ref, out_ref, shifted_ref):
    rows, cols = dmixed_ref.shape
    first = tap_count - 1
    for shift in range(8):
        span = (first - shift) // 8 * 8 + rows
        shifted_ref[shift, pl.ds(0, span), :] = extended_ref[pl.ds(shift, span), :]
    for column in range(cols // 128):
        lanes = pl.ds(column * 128, 128)

        def body(block, sums):
            start = pl.multiple_of(block * 8, 8)
            grads = dmixed_ref[pl.ds(start, 8), lanes]
            updated = []
            for tap in range(tap_count):
                offset, shift = divmod(first - tap, 8)
                window = shifted_ref[shift, pl.ds(pl.multiple_of(start + offset * 8, 8), 8), lanes]
                updated.append(sums[tap] + grads * window)
            return tuple(updated)

        zero = jnp.zeros((8, 128), jnp.float32)
        sums = lax.fori_loop(0, rows // 8, body, tuple(zero for _ in range(tap_count)))
        for tap in range(tap_count):
            out_ref[pl.ds(tap, 1), lanes] = jnp.sum(sums[tap], axis=0, keepdims=True)
    out_ref[pl.ds(tap_count, out_ref.shape[0] - tap_count), :] = jnp.zeros(
        (out_ref.shape[0] - tap_count, out_ref.shape[1]), jnp.float32
    )


def kernel_taps(dmixed, extended, tap_count):
    padded = -(-tap_count // 8) * 8
    return pl.pallas_call(
        functools.partial(kernel_taps_body, tap_count),
        out_shape=jax.ShapeDtypeStruct((padded, dmixed.shape[1]), jnp.float32),
        in_specs=[pl.BlockSpec(memory_space=pltpu.VMEM)] * 2,
        out_specs=pl.BlockSpec(memory_space=pltpu.VMEM),
        scratch_shapes=[pltpu.VMEM((8, dmixed.shape[0] + (tap_count - 1) // 8 * 8, dmixed.shape[1]), jnp.float32)],
    )(dmixed, extended)


def sum_weights(weight_part, kernel_part, kernel_rows):
    weight_total, kernel_total = allreduce(
        [weight_part, kernel_part], lax.axis_size("dp"), lax.axis_size("blk")
    )
    return weight_total, kernel_total[:kernel_rows]


def per_device(queries, key_in, value_in, out_weight, conv_kernel, cotangent):
    cycle_count = lax.axis_size("blk")
    device = lax.axis_index("blk")
    row_count = queries.shape[1]
    context = min(CTX_MAX, cycle_count // 4)
    left_span = context * row_count
    score_scale = 1.0 / math.sqrt(HEAD_DIM)
    edge_rows = conv_kernel.shape[0] - 1
    row_ids = jnp.arange(row_count, dtype=jnp.int32)
    query_heads = split_heads(queries[0])
    own_tile = jnp.concatenate([key_in[0], value_in[0]], axis=1)
    own_pos = device * row_count + row_ids

    offsets = list(range(context, 0, -1))
    window = jnp.concatenate(
        [from_behind(own_tile, "blk", offset) for offset in offsets] + [own_tile], axis=0
    )
    key_pos = jnp.concatenate([(device - offset) * row_count + row_ids for offset in offsets] + [own_pos])
    distance = own_pos[:, None] - key_pos[None, :]
    visible = ((distance >= 0) & (distance < left_span) & (key_pos[None, :] >= 0))[None]
    key_heads = split_heads(window[:, :ATT])
    value_heads = split_heads(window[:, ATT:])

    scores = (
        jnp.einsum("qhd,khd->hqk", query_heads, key_heads, preferred_element_type=jnp.float32)
        * score_scale
    )
    scores = jnp.where(visible, scores, NEGATIVE)
    row_max = jnp.max(scores, axis=-1)
    weights = jnp.where(visible, jnp.exp(scores - row_max[..., None]), 0.0)
    row_sum = jnp.sum(weights, axis=-1)
    weighted = jnp.einsum(
        "hqk,khd->qhd", weights.astype(jnp.bfloat16), value_heads, preferred_element_type=jnp.float32
    )
    attended = (weighted / jnp.transpose(row_sum)[:, :, None]).astype(jnp.bfloat16)
    log_sums = row_max + jnp.log(row_sum)
    flat = attended.reshape(row_count, ATT)

    hidden = jnp.dot(flat, out_weight, preferred_element_type=jnp.float32).astype(jnp.bfloat16)
    before = from_behind(hidden[-edge_rows:], "blk", 1)
    following = from_behind(
        jnp.concatenate([hidden[:edge_rows], cotangent[0][:edge_rows]], axis=1), "blk", -1
    )
    width = hidden.shape[1]
    extended = jnp.concatenate([before, hidden, following[:, :width]], axis=0).astype(jnp.float32)
    mixed_all = depthwise(extended, conv_kernel, row_count + edge_rows, False)
    sigma_all = jax.nn.sigmoid(mixed_all)
    upstream = jnp.concatenate([cotangent[0], following[:, width:]], axis=0).astype(jnp.float32)
    dmixed_all = upstream * sigma_all * (1.0 + mixed_all * (1.0 - sigma_all))
    out_frames = (mixed_all[:row_count] * sigma_all[:row_count]).astype(jnp.bfloat16)[None]
    dmixed = dmixed_all[:row_count]
    dhidden = depthwise(dmixed_all, conv_kernel, row_count, True).astype(jnp.bfloat16)

    kernel_part = kernel_taps(dmixed, extended[: row_count + edge_rows], edge_rows + 1)
    weight_part = jnp.einsum("ra,rd->ad", flat, dhidden, preferred_element_type=jnp.float32)
    weight_total, kernel_total = sum_weights(weight_part, kernel_part, edge_rows + 1)

    dattended = jnp.einsum(
        "rd,ad->ra", dhidden, out_weight, preferred_element_type=jnp.float32
    ).astype(jnp.bfloat16)
    dout_heads = split_heads(dattended)
    deltas = jnp.einsum("rhe,rhe->hr", dout_heads, attended, preferred_element_type=jnp.float32)

    probs = jnp.where(visible, jnp.exp(scores - log_sums[..., None]), 0.0)
    dvalue_heads = jnp.einsum(
        "hqk,qhd->khd", probs.astype(jnp.bfloat16), dout_heads, preferred_element_type=jnp.float32
    )
    dprobs = jnp.einsum("qhd,khd->hqk", dout_heads, value_heads, preferred_element_type=jnp.float32)
    dscores = (probs * (dprobs - deltas[..., None])).astype(jnp.bfloat16)
    dquery = (
        jnp.einsum("hqk,khd->qhd", dscores, key_heads, preferred_element_type=jnp.float32)
        * score_scale
    )
    dkey_heads = (
        jnp.einsum("hqk,qhd->khd", dscores, query_heads, preferred_element_type=jnp.float32)
        * score_scale
    )
    window_rows = window.shape[0]
    dkv = jnp.concatenate(
        [
            dkey_heads.astype(jnp.bfloat16).reshape(window_rows, ATT),
            dvalue_heads.astype(jnp.bfloat16).reshape(window_rows, ATT),
        ],
        axis=1,
    )
    dkv_total = dkv[context * row_count:].astype(jnp.float32)
    for slot, offset in enumerate(offsets):
        part = dkv[slot * row_count:(slot + 1) * row_count]
        dkv_total = dkv_total + from_behind(part, "blk", -offset).astype(jnp.float32)

    query_grad = dquery.reshape(row_count, ATT).astype(jnp.bfloat16)[None]
    key_grad = dkv_total[:, :ATT].astype(jnp.bfloat16)[None]
    value_grad = dkv_total[:, ATT:].astype(jnp.bfloat16)[None]
    return (out_frames, query_grad, key_grad, value_grad, weight_total, kernel_total)


def solution(mesh):
    return jax.shard_map(
        per_device,
        mesh=mesh,
        in_specs=(
            P("dp", "blk", None),
            P("dp", "blk", None),
            P("dp", "blk", None),
            P(),
            P(),
            P("dp", "blk", None),
        ),
        out_specs=(
            P("dp", "blk", None),
            P("dp", "blk", None),
            P("dp", "blk", None),
            P("dp", "blk", None),
            P(),
            P(),
        ),
        check_vma=False,
    )
```
